32 devices in a mesh: dp: 8 (over z, core), tensor: 4 (over y, x).
Axes of the slice: x: 2, y: 2, z: 4, core: 2. Of those that a mesh axis runs over, the one named last changes fastest.
Arguments:
- tokens: bfloat16 [10752, 2048], P(('dp', 'tensor')), may hold values from -6 to 6
- segment: int32 [10752], P('dp'), may hold values from 0 to 31, never falling along the last dimension, each value on 1 to 1344 neighbouring positions
- cotangent: bfloat16 [10752, 2048], P(('dp', 'tensor')), may hold values from -6 to 6
- ln1_gain: float32 [2048], replicated, may hold values from 0.1 to 1.9
- ln1_shift: float32 [2048], replicated, may hold values from -3 to 3
- w_query: float32 [2048, 2048], P('dp', 'tensor'), may hold values from -0.125 to 0.125
- b_query: float32 [2048], P('tensor'), may hold values from -3 to 3
- w_keyval: float32 [2048, 256], P(('dp', 'tensor')), may hold values from -0.125 to 0.125
- b_value: float32 [128], replicated, may hold values from -3 to 3
- w_out: float32 [2048, 2048], P('tensor', 'dp'), may hold values from -1 to 1
- b_out: float32 [2048], replicated, may hold values from -3 to 3
- ln2_gain: float32 [2048], replicated, may hold values from 0.1 to 1.9
- ln2_shift: float32 [2048], replicated, may hold values from -3 to 3
- w_in: float32 [2048, 8192], P('dp', 'tensor'), may hold values from -0.125 to 0.125
- b_in: float32 [8192], P('tensor'), may hold values from -3 to 3
- w_back: float32 [8192, 2048], P('tensor', 'dp'), may hold values from -0.0625 to 0.0625
- b_back: float32 [2048], replicated, may hold values from -3 to 3
Outputs:
- output: bfloat16 [10752, 2048], P(('dp', 'tensor'))
- tokens_grad: bfloat16 [10752, 2048], P(('dp', 'tensor'))
- ln1_gain_grad: float32 [2048], P(('dp', 'tensor'))
- ln1_shift_grad: float32 [2048], P(('dp', 'tensor'))
- w_query_grad: float32 [2048, 2048], P('dp', 'tensor')
- b_query_grad: float32 [2048], P('tensor')
- w_keyval_grad: float32 [2048, 256], P(('dp', 'tensor'))
- b_value_grad: float32 [128], P(('dp', 'tensor'))
- w_out_grad: float32 [2048, 2048], P('tensor', 'dp')
- b_out_grad: float32 [2048], P(('dp', 'tensor'))
- ln2_gain_grad: float32 [2048], P(('dp', 'tensor'))
- ln2_shift_grad: float32 [2048], P(('dp', 'tensor'))
- w_in_grad: float32 [2048, 8192], P('dp', 'tensor')
- b_in_grad: float32 [8192], P('tensor')
- w_back_grad: float32 [8192, 2048], P('tensor', 'dp')
- b_back_grad: float32 [2048], P(('dp', 'tensor'))
The draws below stay inside these ranges and needn't reach their ends.
Inputs may be any that keep to these rules, and one draw needn't show every extreme that they name: `segment`: document numbers never decrease along the tokens; a document has 1 to 1344 tokens and one has exactly 1344.
All inputs are finite; a program needn't handle non-finite values.
Results may differ from the reference program's by a relative error of at most 0.02.
Values may be sent and summed in bfloat16 or wider, within the bound.
A program may use at most 256 MiB of HBM per device.

```python
import math
from functools import partial
import jax
import jax.numpy as jnp
import numpy as np
from jax import lax

D = 2048
HEADS = 16
HD = 128
FF = 8192
LEN = 1344
TOKENS = 10752
DOCS = 32


def level_of(own_key, shape, split, low, top_value):
    def one(position, blocks):
        heights = jax.random.uniform(jax.random.fold_in(jax.random.fold_in(own_key, 6), position), (blocks,), jnp.float32, low / len(split), top_value / len(split))
        return jnp.repeat(jnp.exp(heights), shape[position] // blocks).reshape((-1,) + (1,) * (len(shape) - position - 1))

    level = one(*split[0])
    for cut in split[1:]:
        level = level * one(*cut)
    return level


def length_profile(amount, total, most, slope):
    weights = [(1 << 20) // math.isqrt(grade ** slope) + 1 for grade in range(2, amount + 1)]
    spare, holding = total - most - (amount - 1), [1] * (amount - 1)
    while spare > 0:
        movable = [i for i in range(amount - 1) if holding[i] < most]
        whole, remaining = sum([weights[i] for i in movable]), spare
        for i in movable:
            addition = min(most - holding[i], max(1, remaining * weights[i] // whole), spare)
            holding[i] = holding[i] + addition
            spare = spare - addition
    return np.array([most] + holding)


def ragged(own_key, count, total, limit, slope):
    if count == 2:
        one = jax.random.randint(own_key, (), max(1, total - limit), min(limit, total - 1) + 1)
        return jnp.stack([one, total - one])
    tallies = jnp.asarray(length_profile(count, total, limit, slope), jnp.int32)
    couples = (count - 1) // 2
    donor, receiver = tallies[1:1 + 2 * couples:2], tallies[2:2 + 2 * couples:2]
    slack = jnp.minimum(donor - 1, limit - receiver)
    shifted = jax.random.randint(jax.random.fold_in(own_key, 1), (couples,), 0, 1 << 20) % (slack + 1)
    tallies = tallies.at[1:1 + 2 * couples:2].set(donor - shifted).at[2:2 + 2 * couples:2].set(receiver + shifted)
    return tallies[jax.random.permutation(jax.random.fold_in(own_key, 2), count)]


def noise(rng, shape, width, limit, split=(), held_as=jnp.bfloat16):
    array = jax.random.normal(rng, shape, jnp.float32) * width
    if len(split) > 0:
        array = level_of(rng, shape, split, -0.22, 0.18) * array
    return jnp.clip(array, min=-limit, max=limit).astype(held_as)


def setup_inputs(seed: int = 0) -> dict:
    keys = jax.random.split(jax.random.key(seed), 18)
    return {
        "tokens": noise(keys[0], (TOKENS, D), 1.0, 6.0, ((0, 32),)),
        "segment": jnp.searchsorted(jnp.cumsum(ragged(keys[1], DOCS, TOKENS, LEN, 2)), jnp.arange(TOKENS), side="right").astype(jnp.int32),
        "cotangent": noise(keys[2], (TOKENS, D), 1.0, 6.0, ((0, 32),)),
        "ln1_gain": jnp.clip(1.0 + 0.18 * jax.random.normal(keys[3], (D,), jnp.float32), 0.1, 1.9),
        "ln1_shift": noise(keys[4], (D,), 0.5, 3.0, (), jnp.float32),
        "w_query": noise(keys[5], (D, HEADS * HD), D ** -0.5, 0.125, ((0, 8), (1, 4)), jnp.float32),
        "b_query": noise(keys[6], (HEADS * HD,), 0.5, 3.0, ((0, 4),), jnp.float32),
        "w_keyval": noise(keys[7], (D, 2 * HD), D ** -0.5, 0.125, ((0, 32),), jnp.float32),
        "b_value": noise(keys[8], (HD,), 0.5, 3.0, (), jnp.float32),
        "w_out": noise(keys[9], (HEADS * HD, D), (HEADS * HD // 64) ** -0.5, 1.0, ((0, 4), (1, 8)), jnp.float32),
        "b_out": noise(keys[10], (D,), 0.5, 3.0, (), jnp.float32),
        "ln2_gain": jnp.clip(1.0 + 0.18 * jax.random.normal(keys[11], (D,), jnp.float32), 0.1, 1.9),
        "ln2_shift": noise(keys[12], (D,), 0.5, 3.0, (), jnp.float32),
        "w_in": noise(keys[13], (D, FF), D ** -0.5, 0.125, ((0, 8), (1, 4)), jnp.float32),
        "b_in": noise(keys[14], (FF,), 0.5, 3.0, ((0, 4),), jnp.float32),
        "w_back": noise(keys[15], (FF, D), FF ** -0.5, 0.0625, ((0, 4), (1, 8)), jnp.float32),
        "b_back": noise(keys[16], (D,), 0.5, 3.0, (), jnp.float32),
    }


@jax.custom_vjp
def low(v):
    return lax.optimization_barrier(v.astype(jnp.bfloat16)).astype(jnp.float32)

@jax.custom_vjp
def low_back(v):
    return v

def low_keep(v):
    return (low(v), None)

def low_pass(kept, grad):
    return (grad,)

def back_keep(v):
    return (v, None)

def back_low(kept, grad):
    return (low(grad),)
low.defvjp(low_keep, low_pass)
low_back.defvjp(back_keep, back_low)

def round_both(values):
    return low(low_back(values))

def product(left, right):
    return jnp.dot(left, right, precision=lax.Precision.HIGHEST)

def layer_norm(inputs, norm_gain, norm_shift):
    average = lax.optimization_barrier(jnp.mean(inputs, axis=-1, keepdims=True))
    centered = inputs - average
    variance = lax.optimization_barrier(jnp.mean(centered * centered, axis=-1, keepdims=True))
    return centered * lax.rsqrt(variance + 1e-05) * norm_gain + norm_shift

def attend(inputs):
    queries, keys_seq, values_seq, seg_ids = inputs
    scores = jnp.einsum('qhd,kd->hqk', queries, keys_seq, precision=lax.Precision.HIGHEST) * (1.0 / math.sqrt(HD))
    scores = low_back(scores)
    places = jnp.arange(LEN, dtype=jnp.int32)
    allowed = (seg_ids[:, None] == seg_ids[None, :]) & (places[:, None] >= places[None, :])
    scores = jnp.where(allowed[None], scores, -1e+30)
    weights = jax.nn.softmax(scores, axis=-1)
    return jnp.einsum('hqk,kd->qhd', low(weights), values_seq, precision=lax.Precision.HIGHEST)

def forward(segment, inputs, ln1_gain, ln1_shift, w_query, b_query, w_keyval, b_value, w_out, b_out, ln2_gain, ln2_shift, w_in, b_in, w_back, b_back):
    normed = low(layer_norm(inputs, ln1_gain, ln1_shift))
    queries = round_both(product(normed, low(w_query)) + b_query)
    keyval = product(normed, low(w_keyval))
    keys_all = round_both(keyval[:, :HD])
    values_all = round_both(keyval[:, HD:] + b_value)
    seq_count = TOKENS // LEN
    mixture = lax.map(jax.checkpoint(attend), (queries.reshape(seq_count, LEN, HEADS, HD), keys_all.reshape(seq_count, LEN, HD), values_all.reshape(seq_count, LEN, HD), segment.reshape(seq_count, LEN)))
    mixture = round_both(mixture.reshape(TOKENS, HEADS * HD))
    hidden = inputs + low_back(product(mixture, low(w_out))) + b_out
    normed_two = low(layer_norm(hidden, ln2_gain, ln2_shift))
    pre_gelu = low_back(product(normed_two, low(w_in)) + b_in)
    activated = low(jax.nn.gelu(pre_gelu, approximate=True))
    return hidden + low_back(product(activated, low(w_back))) + b_back

def reference(tokens, segment, cotangent, ln1_gain, ln1_shift, w_query, b_query, w_keyval, b_value, w_out, b_out, ln2_gain, ln2_shift, w_in, b_in, w_back, b_back):
    result, pull = jax.vjp(partial(forward, segment), tokens.astype(jnp.float32), ln1_gain, ln1_shift, w_query, b_query, w_keyval, b_value, w_out, b_out, ln2_gain, ln2_shift, w_in, b_in, w_back, b_back)
    grads = pull(cotangent.astype(jnp.float32))
    return (result.astype(jnp.bfloat16), grads[0].astype(jnp.bfloat16), grads[1], grads[2], grads[3], grads[4], grads[5], grads[6], grads[7], grads[8], grads[9], grads[10], grads[11], grads[12], grads[13], grads[14])
```

```python
import functools
import math

import jax
import jax.numpy as jnp
from jax import lax
from jax.experimental import pallas as pl
from jax.experimental.pallas import tpu as pltpu
from jax.sharding import PartitionSpec as P

LEN = 1344
HD = 128
QB = 112
KB = 224
SCALE = 1.0 / math.sqrt(HD)
EXP2 = SCALE * math.log2(math.e)
NEG = -1e30
BF = jnp.bfloat16
F32 = jnp.float32


def _stack(ref, heads):
    return jnp.concatenate([ref[0, :, h * HD : (h + 1) * HD] for h in range(heads)], axis=0)


def _allowed(info_ref, first):
    shape = (KB, info_ref.shape[2])
    place = lax.broadcasted_iota(jnp.int32, shape, 0) + first
    return (place >= info_ref[0, 0:1, :]) & (place <= info_ref[0, 1:2, :])


def _nt(a, b):
    return lax.dot_general(a, b, (((1,), (1,)), ((), ())), preferred_element_type=F32)


def attend_kernel(heads, place_ref, low_ref, top_ref, q_ref, k_ref, vt_ref, info_ref, o_ref, lse_ref, s_ref):
    step = pl.program_id(0)
    low, top = low_ref[step], top_ref[step]
    q = _stack(q_ref, heads)
    rows = q.shape[0]

    def score(c, best):
        s = _nt(k_ref[0, pl.ds(pl.multiple_of(c * KB, KB), KB), :], q)
        s = jnp.where(_allowed(info_ref, c * KB), s, NEG)
        s_ref[c] = s
        return jnp.maximum(best, jnp.max(s, axis=0, keepdims=True))

    best = lax.fori_loop(low, top, score, jnp.full((1, rows), NEG, F32))
    shift = best * EXP2

    def mix(c, carry):
        total, acc = carry
        p = jnp.exp2(s_ref[c] * EXP2 - shift)
        total = total + jnp.sum(p, axis=0, keepdims=True)
        acc = acc + jnp.dot(vt_ref[0, c], p.astype(BF), preferred_element_type=F32)
        return total, acc

    total, acc = lax.fori_loop(
        low, top, mix, (jnp.zeros((1, rows), F32), jnp.zeros((HD, rows), F32))
    )
    out = (acc / total).T.astype(BF)
    for h in range(heads):
        o_ref[0, :, h * HD : (h + 1) * HD] = out[h * QB : (h + 1) * QB]
    lse_ref[0] = jnp.broadcast_to(shift + jnp.log2(total), lse_ref.shape[1:])


def attend_back_kernel(
    heads, per_seq, place_ref, low_ref, top_ref, q_ref, o_ref, do_ref, k_ref, v_ref, kt_ref, info_ref, lse_ref,
    dq_ref, dkv_ref, dk_acc, dv_acc,
):
    step = pl.program_id(0)
    inner = lax.rem(step, per_seq)
    low, top = low_ref[step], top_ref[step]

    @pl.when(inner == 0)
    def _():
        dk_acc[...] = jnp.zeros_like(dk_acc)
        dv_acc[...] = jnp.zeros_like(dv_acc)

    q = _stack(q_ref, heads)
    do = _stack(do_ref, heads)
    rows = q.shape[0]
    prod = do.astype(F32) * _stack(o_ref, heads).astype(F32)
    delta = jnp.sum(prod.T, axis=0, keepdims=True)
    lse = lse_ref[0, 0:1, :]

    def body(c, acc):
        window = pl.ds(pl.multiple_of(c * KB, KB), KB)
        s = _nt(k_ref[0, window, :], q)
        s = jnp.where(_allowed(info_ref, c * KB), s * EXP2 - lse, NEG)
        p = jnp.exp2(s)
        dp = _nt(v_ref[0, window, :], do)
        ds = (p * (dp - delta)).astype(BF)
        dv_acc[window, :] += jnp.dot(p.astype(BF), do, preferred_element_type=F32)
        dk_acc[window, :] += jnp.dot(ds, q, preferred_element_type=F32)
        return acc + jnp.dot(kt_ref[0, c], ds, preferred_element_type=F32)

    acc = lax.fori_loop(low, top, body, jnp.zeros((HD, rows), F32))
    dq = (acc * SCALE).T.astype(BF)
    for h in range(heads):
        dq_ref[0, :, h * HD : (h + 1) * HD] = dq[h * QB : (h + 1) * QB]

    @pl.when(inner == per_seq - 1)
    def _():
        dkv_ref[0, :, :HD] = (dk_acc[...] * SCALE).astype(BF)
        dkv_ref[0, :, HD:] = dv_acc[...].astype(BF)


class Attention:
    def __init__(self, segment, place, rows, heads):
        self.heads, self.rows = heads, rows
        self.seqs = segment.shape[0] // LEN
        self.per_seq = LEN // QB
        self.per_block = rows // QB
        self.steps = self.seqs * self.per_seq
        self.place = place
        seg = segment.reshape(self.seqs, LEN)
        start = jnp.sum((seg[:, None, :] < seg[:, :, None]).astype(jnp.int32), axis=-1)
        pos = jnp.broadcast_to(jnp.arange(LEN, dtype=jnp.int32), seg.shape)
        info = jnp.stack([start, pos], axis=1).reshape(self.seqs, 2, self.per_seq, 1, QB)
        info = jnp.broadcast_to(info, (self.seqs, 2, self.per_seq, heads, QB))
        self.info = info.transpose(0, 2, 1, 3, 4).reshape(self.steps, 2, heads * QB)
        self.low = start.reshape(self.steps, QB)[:, 0] // KB
        last = pos.reshape(self.steps, QB)[:, -1]
        self.top = last // KB + 1

    def _specs(self):
        per_seq, per_block, heads = self.per_seq, self.per_block, self.heads
        wide = heads * HD
        query = pl.BlockSpec((1, QB, wide), lambda i, place, *_: (place[i // per_block], i % per_block, 0))
        key = pl.BlockSpec((1, LEN, HD), lambda i, *_: (i // per_seq, 0, 0))
        keyt = pl.BlockSpec((1, LEN // KB, HD, KB), lambda i, *_: (i // per_seq, 0, 0, 0))
        info = pl.BlockSpec((1, 2, heads * QB), lambda i, *_: (i, 0, 0))
        lse = pl.BlockSpec((1, 8, heads * QB), lambda i, *_: (i, 0, 0))
        return query, key, keyt, info, lse

    def _cost(self, products):
        pairs = self.steps * QB * self.heads * LEN // 2
        return pl.CostEstimate(
            flops=2 * pairs * HD * products, transcendentals=pairs, bytes_accessed=8 * self.steps * QB * HD * self.heads
        )

    def forward(self, q, keys, values_t):
        query, key, keyt, info, lse = self._specs()
        lanes = self.heads * QB
        return pl.pallas_call(
            functools.partial(attend_kernel, self.heads),
            grid_spec=pltpu.PrefetchScalarGridSpec(
                num_scalar_prefetch=3,
                grid=(self.steps,),
                in_specs=[query, key, keyt, info],
                out_specs=[query, lse],
                scratch_shapes=[pltpu.VMEM((LEN // KB, KB, lanes), F32)],
            ),
            out_shape=[
                jax.ShapeDtypeStruct(q.shape, BF),
                jax.ShapeDtypeStruct((self.steps, 8, lanes), F32),
            ],
            cost_estimate=self._cost(2),
            name="attend",
        )(self.place, self.low, self.top, q, keys, values_t, self.info)

    def backward(self, q, o, do, keys, values, keys_t, lse_in):
        query, key, keyt, info, lse = self._specs()
        per_seq = self.per_seq
        return pl.pallas_call(
            functools.partial(attend_back_kernel, self.heads, per_seq),
            grid_spec=pltpu.PrefetchScalarGridSpec(
                num_scalar_prefetch=3,
                grid=(self.steps,),
                in_specs=[query, query, query, key, key, keyt, info, lse],
                out_specs=[query, pl.BlockSpec((1, LEN, 2 * HD), lambda i, *_: (i // per_seq, 0, 0))],
                scratch_shapes=[pltpu.VMEM((LEN, HD), F32), pltpu.VMEM((LEN, HD), F32)],
            ),
            out_shape=[
                jax.ShapeDtypeStruct(q.shape, BF),
                jax.ShapeDtypeStruct((self.seqs, LEN, 2 * HD), BF),
            ],
            cost_estimate=self._cost(5),
            name="attend_back",
        )(self.place, self.low, self.top, q, o, do, keys, values, keys_t, self.info, lse_in)


def key_chunks(keys):
    seqs = keys.shape[0]
    return keys.reshape(seqs, LEN // KB, KB, HD).transpose(0, 1, 3, 2)


def _hop(v, axis, mask):
    size = lax.axis_size(axis)
    return lax.ppermute(v, axis, [(i, i ^ mask) for i in range(size)])


def _half(rows):
    return rows // 2 // 16 * 16


class Square:
    def __init__(self, blocks):
        self.count = blocks
        me = lax.axis_index("tensor")
        self.place = me ^ jnp.arange(blocks, dtype=jnp.int32)

    def gather(self, v):
        h = _half(v.shape[0])
        bx, by = _hop(v, "tensor", 1), _hop(v, "tensor", 2)
        top, bottom = _hop(by[:h], "tensor", 1), _hop(bx[h:], "tensor", 2)
        return [v, bx, by, jnp.concatenate([top, bottom], axis=0)]

    def scatter(self, make):
        corner = make(3).astype(BF)
        h = _half(corner.shape[0])
        to_y, to_x = _hop(corner[:h], "tensor", 1), _hop(corner[h:], "tensor", 2)
        zero = [(0, 0)] * (corner.ndim - 1)
        py = make(2) + jnp.pad(to_y.astype(F32), [(0, corner.shape[0] - h)] + zero)
        px = make(1) + jnp.pad(to_x.astype(F32), [(h, 0)] + zero)
        ry, rx = _hop(py.astype(BF), "tensor", 2), _hop(px.astype(BF), "tensor", 1)
        return make(0) + rx.astype(F32) + ry.astype(F32)

    def ordered(self, stacked):
        return jnp.take(stacked, self.place, axis=0, mode="clip")

    def relative(self, stacked):
        return jnp.take(stacked, self.place, axis=0, mode="clip")


class Plain:
    def __init__(self, blocks):
        self.count = blocks
        self.place = jnp.arange(blocks, dtype=jnp.int32)

    def gather(self, v):
        whole = lax.all_gather(v, "tensor", axis=0)
        return [whole[i] for i in range(self.count)]

    def scatter(self, make):
        whole = jnp.concatenate([make(i).astype(BF) for i in range(self.count)], axis=0)
        return lax.psum_scatter(whole, "tensor", scatter_dimension=0, tiled=True).astype(F32)

    def ordered(self, stacked):
        return stacked

    def relative(self, stacked):
        return stacked


def after(value, *others):
    return lax.optimization_barrier((value, others))[0]


def total_over(v, *axes):
    for axis in axes:
        mask = 1
        while mask < lax.axis_size(axis):
            v = v + _hop(v, axis, mask)
            mask *= 2
    return v


def norm_parts(v):
    average = jnp.mean(v, axis=-1, keepdims=True)
    centered = v - average
    rate = lax.rsqrt(jnp.mean(centered * centered, axis=-1, keepdims=True) + 1e-05)
    return centered * rate, rate


def norm_back(grad, hat, rate, gain):
    scaled = grad * gain
    return rate * (
        scaled
        - jnp.mean(scaled, axis=-1, keepdims=True)
        - hat * jnp.mean(scaled * hat, axis=-1, keepdims=True)
    )


GELU_A = math.sqrt(2.0 / math.pi)
GELU_B = 0.044715


def gelu_both(a):
    square = a * a
    t = jnp.tanh(GELU_A * (a + GELU_B * square * a))
    half = 0.5 * (1.0 + t)
    slope = half + 0.5 * a * (1.0 - t * t) * (GELU_A * (1.0 + 3.0 * GELU_B * square))
    return a * half, slope


def dot(a, b):
    return jnp.dot(a, b, preferred_element_type=F32)


def dot_t(a, b):
    return lax.dot_general(a, b, (((1,), (1,)), ((), ())), preferred_element_type=F32)


def dot_tokens(a, b):
    return lax.dot_general(a, b, (((0,), (0,)), ((), ())), preferred_element_type=F32)


def per_device(
    tokens,
    segment,
    cotangent,
    ln1_gain,
    ln1_shift,
    w_query,
    b_query,
    w_keyval,
    b_value,
    w_out,
    b_out,
    ln2_gain,
    ln2_shift,
    w_in,
    b_in,
    w_back,
    b_back,
):
    dp, nt = lax.axis_size("dp"), lax.axis_size("tensor")
    me_dp, me_t = lax.axis_index("dp"), lax.axis_index("tensor")
    rows, width = tokens.shape
    heads = b_query.shape[0] // HD
    wide = heads * HD
    inputs = tokens.astype(F32)
    net = Square(nt) if nt == 4 else Plain(nt)

    kv_rows = w_keyval.size // wide
    out_rows = w_out.size // wide
    pack = jnp.concatenate(
        [
            w_query.astype(BF),
            w_keyval.astype(BF).reshape(kv_rows, wide),
            w_out.astype(BF).reshape(out_rows, wide),
        ],
        axis=0,
    )
    packed = lax.all_gather(pack, "dp", axis=0)
    query_full = packed[:, : w_query.shape[0]].reshape(width, wide)
    keyval_own = packed[:, w_query.shape[0] : w_query.shape[0] + kv_rows]
    output_full = (
        packed[:, w_query.shape[0] + kv_rows :]
        .reshape(dp, wide, w_out.shape[1])
        .transpose(1, 0, 2)
        .reshape(wide, width)
    )
    inner_full = lax.all_gather(w_in.astype(BF), "dp", axis=0, tiled=True)
    down_full = lax.all_gather(w_back.astype(BF), "dp", axis=1, tiled=True)
    keyval_own = keyval_own.reshape(dp * w_keyval.shape[0], 2 * HD)
    keyval_all = net.ordered(jnp.stack(net.gather(keyval_own)))
    keyval_full = (
        keyval_all.reshape(nt, dp, w_keyval.shape[0], 2 * HD).transpose(1, 0, 2, 3).reshape(width, 2 * HD)
    )

    hat1, rate1 = norm_parts(inputs)
    normed1 = (hat1 * ln1_gain + ln1_shift).astype(BF)
    n1 = net.gather(normed1)
    cot = net.gather(after(cotangent, n1[-1]))
    queries = jnp.stack([(dot(n, query_full) + b_query).astype(BF) for n in n1])
    bias = jnp.concatenate([jnp.zeros_like(b_value), b_value])
    keyval = jnp.stack(net.gather((dot(normed1, keyval_full) + bias).astype(BF)))
    seqs = nt * rows // LEN
    keyval = net.ordered(keyval).reshape(seqs, LEN, 2 * HD)
    keys, values = keyval[..., :HD], keyval[..., HD:]
    attention = Attention(segment, net.place, rows, heads)
    mixture, lse = attention.forward(queries, keys, key_chunks(values))
    mixture = after(mixture, cot[-1])
    attended = net.scatter(lambda i: dot(mixture[i], output_full))
    hidden = inputs + attended + b_out

    hat2, rate2 = norm_parts(hidden)
    normed2 = (hat2 * ln2_gain + ln2_shift).astype(BF)
    n2 = net.gather(normed2)
    act, slope = [], []
    for n in n2:
        a, g = gelu_both(dot(n, inner_full) + b_in)
        act.append(a.astype(BF))
        slope.append(g.astype(BF))
    cot_all = jnp.concatenate(cot, axis=0)
    act_all = jnp.concatenate(act, axis=0)
    down_grad = dot_tokens(act_all, cot_all).astype(BF)
    down_total = lax.psum_scatter(down_grad, "dp", scatter_dimension=1, tiled=True).astype(F32)
    down_full = after(down_full, down_grad)
    pre_grad = [(dot_t(c, down_full) * g.astype(F32)).astype(BF) for c, g in zip(cot, slope)]
    second_grad = net.scatter(lambda i: dot_t(pre_grad[i], inner_full))
    pre_all = jnp.concatenate(pre_grad, axis=0)
    inner_grad = dot_tokens(jnp.concatenate(n2, axis=0), pre_all).astype(BF)
    inner_total = lax.psum_scatter(after(inner_grad, down_total), "dp", scatter_dimension=0, tiled=True).astype(F32)
    inner_bias = jnp.sum(pre_all, axis=0, dtype=F32)
    second_grad = after(second_grad, inner_grad)

    act = after(act, second_grad)
    feed = net.scatter(lambda i: dot(act[i], down_full))
    output = (hidden + feed + b_back).astype(BF)

    grad_out = cotangent.astype(F32)
    hidden_grad = grad_out + norm_back(second_grad, hat2, rate2, ln2_gain)
    hid = net.gather(hidden_grad.astype(BF))
    mixture_grad = jnp.stack([dot_t(h, output_full).astype(BF) for h in hid])
    query_low, keyval_part = attention.backward(
        queries, mixture, after(mixture_grad, down_total), keys, values, key_chunks(keys), lse
    )
    output_grad = dot_tokens(mixture.reshape(nt * rows, wide), jnp.concatenate(hid, axis=0)).astype(BF)
    output_total = lax.psum_scatter(after(output_grad, inner_total), "dp", scatter_dimension=1, tiled=True).astype(F32)
    query_grad = dot_tokens(jnp.concatenate(n1, axis=0), query_low.reshape(nt * rows, wide)).astype(BF)
    query_bias = jnp.sum(query_low, axis=(0, 1), dtype=F32)

    parts = net.relative(keyval_part.reshape(nt, rows, 2 * HD))
    keyval_low = net.scatter(lambda i: parts[i].astype(F32)).astype(BF)
    normed_grad = net.scatter(lambda i: dot_t(query_low[i], query_full)) + dot_t(keyval_low, keyval_full)
    keyval_grad = dot_tokens(normed1, keyval_low).reshape(dp, nt, w_keyval.shape[0], 2 * HD)
    keyval_grad = keyval_grad.transpose(1, 0, 2, 3).reshape(nt, dp * w_keyval.shape[0], 2 * HD)
    keyval_grad = net.relative(keyval_grad)
    keyval_grad = net.scatter(lambda i: keyval_grad[i]).astype(BF)
    query_pack = jnp.concatenate(
        [query_grad.reshape(dp, w_query.shape[0], wide), keyval_grad.reshape(dp, kv_rows, wide)], axis=1
    )
    query_total = lax.psum_scatter(after(query_pack, output_total), "dp", scatter_dimension=0, tiled=True)[0].astype(F32)
    keyval_total = query_total[w_query.shape[0] :].reshape(w_keyval.shape)
    query_total = query_total[: w_query.shape[0]]

    normed_grad = after(normed_grad, inner_total)
    tokens_grad = (hidden_grad + norm_back(normed_grad, hat1, rate1, ln1_gain)).astype(BF)

    early = jnp.concatenate(
        [
            jnp.sum(second_grad * hat2, axis=0),
            jnp.sum(second_grad, axis=0),
            jnp.sum(hidden_grad, axis=0),
            jnp.sum(grad_out, axis=0),
        ]
    )
    early = total_over(early.reshape(-1, 128), "tensor", "dp").reshape(4, width)
    local = total_over(jnp.concatenate([inner_bias, query_bias]).reshape(-1, 128), "dp").reshape(-1)
    late = jnp.concatenate(
        [
            jnp.sum(normed_grad * hat1, axis=0),
            jnp.sum(normed_grad, axis=0),
            jnp.sum(keyval_low[:, HD:], axis=0, dtype=F32),
        ]
    )
    late = total_over(late.reshape(-1, 128), "tensor", "dp").reshape(-1)
    me = me_dp * nt + me_t

    def own(v):
        part = v.shape[-1] // (dp * nt)
        return lax.dynamic_slice_in_dim(v, me * part, part, axis=v.ndim - 1)

    early = own(early)
    return (
        output,
        tokens_grad,
        own(late[:width]),
        own(late[width : 2 * width]),
        query_total,
        local[b_in.shape[0] :],
        keyval_total,
        own(late[2 * width :]),
        output_total,
        early[2],
        early[0],
        early[1],
        inner_total,
        local[: b_in.shape[0]],
        down_total,
        early[3],
    )


def solution(mesh):
    return jax.shard_map(
        per_device,
        mesh=mesh,
        in_specs=(
            P(("dp", "tensor"), None),
            P("dp"),
            P(("dp", "tensor"), None),
            P(),
            P(),
            P("dp", "tensor"),
            P("tensor"),
            P(("dp", "tensor"), None),
            P(),
            P("tensor", "dp"),
            P(),
            P(),
            P(),
            P("dp", "tensor"),
            P("tensor"),
            P("tensor", "dp"),
            P(),
        ),
        out_specs=(
            P(("dp", "tensor"), None),
            P(("dp", "tensor"), None),
            P(("dp", "tensor")),
            P(("dp", "tensor")),
            P("dp", "tensor"),
            P("tensor"),
            P(("dp", "tensor"), None),
            P(("dp", "tensor")),
            P("tensor", "dp"),
            P(("dp", "tensor")),
            P(("dp", "tensor")),
            P(("dp", "tensor")),
            P("dp", "tensor"),
            P("tensor"),
            P("tensor", "dp"),
            P(("dp", "tensor")),
        ),
        check_vma=False,
    )
```

```python
import functools
import math

import jax
import jax.numpy as jnp
from jax import lax
from jax.experimental import pallas as pl
from jax.experimental.pallas import tpu as pltpu
from jax.sharding import PartitionSpec as P

LEN = 1344
HD = 128
QB = 112
KB = 224
SCALE = 1.0 / math.sqrt(HD)
EXP2 = SCALE * math.log2(math.e)
NEG = -1e30
BF = jnp.bfloat16
F32 = jnp.float32


def _stack(ref, heads):
    return jnp.concatenate([ref[0, :, h * HD : (h + 1) * HD] for h in range(heads)], axis=0)


def _allowed(info_ref, first):
    shape = (KB, info_ref.shape[2])
    place = lax.broadcasted_iota(jnp.int32, shape, 0) + first
    return (place >= info_ref[0, 0:1, :]) & (place <= info_ref[0, 1:2, :])


def _nt(a, b):
    return lax.dot_general(a, b, (((1,), (1,)), ((), ())), preferred_element_type=F32)


def _turn(ref, out):
    for c in range(LEN // KB):
        out[c] = ref[0, c * KB : (c + 1) * KB, :].astype(F32).T.astype(BF)


def attend_kernel(
    heads, per_seq, place_ref, low_ref, top_ref, q_ref, k_ref, v_ref, info_ref, o_ref, lse_ref, s_ref, vt_ref
):
    step = pl.program_id(0)
    low, top = low_ref[step], top_ref[step]

    @pl.when(lax.rem(step, per_seq) == 0)
    def _():
        _turn(v_ref, vt_ref)

    q = _stack(q_ref, heads)
    rows = q.shape[0]

    def score(c, best):
        s = _nt(k_ref[0, pl.ds(pl.multiple_of(c * KB, KB), KB), :], q)
        s = jnp.where(_allowed(info_ref, c * KB), s, NEG)
        s_ref[c] = s
        return jnp.maximum(best, jnp.max(s, axis=0, keepdims=True))

    best = lax.fori_loop(low, top, score, jnp.full((1, rows), NEG, F32))
    shift = best * EXP2

    def mix(c, carry):
        total, acc = carry
        p = jnp.exp2(s_ref[c] * EXP2 - shift)
        total = total + jnp.sum(p, axis=0, keepdims=True)
        acc = acc + jnp.dot(vt_ref[c], p.astype(BF), preferred_element_type=F32)
        return total, acc

    total, acc = lax.fori_loop(
        low, top, mix, (jnp.zeros((1, rows), F32), jnp.zeros((HD, rows), F32))
    )
    out = (acc / total).T.astype(BF)
    for h in range(heads):
        o_ref[0, :, h * HD : (h + 1) * HD] = out[h * QB : (h + 1) * QB]
    lse_ref[0] = jnp.broadcast_to(shift + jnp.log2(total), lse_ref.shape[1:])


def attend_back_kernel(
    heads, per_seq, place_ref, low_ref, top_ref, q_ref, o_ref, do_ref, k_ref, v_ref, info_ref, lse_ref,
    dq_ref, dkv_ref, dk_acc, dv_acc, kt_ref,
):
    step = pl.program_id(0)
    inner = lax.rem(step, per_seq)
    low, top = low_ref[step], top_ref[step]

    @pl.when(inner == 0)
    def _():
        dk_acc[...] = jnp.zeros_like(dk_acc)
        dv_acc[...] = jnp.zeros_like(dv_acc)
        _turn(k_ref, kt_ref)

    q = _stack(q_ref, heads)
    do = _stack(do_ref, heads)
    rows = q.shape[0]
    prod = do.astype(F32) * _stack(o_ref, heads).astype(F32)
    delta = jnp.sum(prod.T, axis=0, keepdims=True)
    lse = lse_ref[0, 0:1, :]

    def body(c, acc):
        window = pl.ds(pl.multiple_of(c * KB, KB), KB)
        s = _nt(k_ref[0, window, :], q)
        s = jnp.where(_allowed(info_ref, c * KB), s * EXP2 - lse, NEG)
        p = jnp.exp2(s)
        dp = _nt(v_ref[0, window, :], do)
        ds = (p * (dp - delta)).astype(BF)
        dv_acc[window, :] += jnp.dot(p.astype(BF), do, preferred_element_type=F32)
        dk_acc[window, :] += jnp.dot(ds, q, preferred_element_type=F32)
        return acc + jnp.dot(kt_ref[c], ds, preferred_element_type=F32)

    acc = lax.fori_loop(low, top, body, jnp.zeros((HD, rows), F32))
    dq = (acc * SCALE).T.astype(BF)
    for h in range(heads):
        dq_ref[0, :, h * HD : (h + 1) * HD] = dq[h * QB : (h + 1) * QB]

    @pl.when(inner == per_seq - 1)
    def _():
        dkv_ref[0, :, :HD] = (dk_acc[...] * SCALE).astype(BF)
        dkv_ref[0, :, HD:] = dv_acc[...].astype(BF)


class Attention:
    def __init__(self, segment, place, rows, heads):
        self.heads, self.rows = heads, rows
        self.seqs = segment.shape[0] // LEN
        self.per_seq = LEN // QB
        self.per_block = rows // QB
        self.steps = self.seqs * self.per_seq
        self.place = place
        seg = segment.reshape(self.seqs, LEN)
        start = jnp.sum((seg[:, None, :] < seg[:, :, None]).astype(jnp.int32), axis=-1)
        pos = jnp.broadcast_to(jnp.arange(LEN, dtype=jnp.int32), seg.shape)
        info = jnp.stack([start, pos], axis=1).reshape(self.seqs, 2, self.per_seq, 1, QB)
        info = jnp.broadcast_to(info, (self.seqs, 2, self.per_seq, heads, QB))
        self.info = info.transpose(0, 2, 1, 3, 4).reshape(self.steps, 2, heads * QB)
        self.low = start.reshape(self.steps, QB)[:, 0] // KB
        last = pos.reshape(self.steps, QB)[:, -1]
        self.top = last // KB + 1

    def _specs(self):
        per_seq, per_block, heads = self.per_seq, self.per_block, self.heads
        wide = heads * HD
        query = pl.BlockSpec((1, QB, wide), lambda i, place, *_: (place[i // per_block], i % per_block, 0))
        key = pl.BlockSpec((1, LEN, HD), lambda i, *_: (i // per_seq, 0, 0))
        value = pl.BlockSpec((1, LEN, HD), lambda i, *_: (i // per_seq, 0, 1))
        info = pl.BlockSpec((1, 2, heads * QB), lambda i, *_: (i, 0, 0))
        lse = pl.BlockSpec((1, 8, heads * QB), lambda i, *_: (i, 0, 0))
        return query, key, value, info, lse

    def _cost(self, products):
        pairs = self.steps * QB * self.heads * LEN // 2
        return pl.CostEstimate(
            flops=2 * pairs * HD * products, transcendentals=pairs, bytes_accessed=8 * self.steps * QB * HD * self.heads
        )

    def forward(self, q, keyval):
        query, key, value, info, lse = self._specs()
        lanes = self.heads * QB
        return pl.pallas_call(
            functools.partial(attend_kernel, self.heads, self.per_seq),
            grid_spec=pltpu.PrefetchScalarGridSpec(
                num_scalar_prefetch=3,
                grid=(self.steps,),
                in_specs=[query, key, value, info],
                out_specs=[query, lse],
                scratch_shapes=[pltpu.VMEM((LEN // KB, KB, lanes), F32), pltpu.VMEM((LEN // KB, HD, KB), BF)],
            ),
            out_shape=[
                jax.ShapeDtypeStruct((*q.shape[:2], self.heads * HD), BF),
                jax.ShapeDtypeStruct((self.steps, 8, lanes), F32),
            ],
            cost_estimate=self._cost(2),
            name="attend",
        )(self.place, self.low, self.top, q, keyval, keyval, self.info)

    def backward(self, q, o, do, keyval, lse_in):
        query, key, value, info, lse = self._specs()
        per_seq = self.per_seq
        return pl.pallas_call(
            functools.partial(attend_back_kernel, self.heads, per_seq),
            grid_spec=pltpu.PrefetchScalarGridSpec(
                num_scalar_prefetch=3,
                grid=(self.steps,),
                in_specs=[query, query, query, key, value, info, lse],
                out_specs=[query, pl.BlockSpec((1, LEN, 2 * HD), lambda i, *_: (i // per_seq, 0, 0))],
                scratch_shapes=[
                    pltpu.VMEM((LEN, HD), F32),
                    pltpu.VMEM((LEN, HD), F32),
                    pltpu.VMEM((LEN // KB, HD, KB), BF),
                ],
            ),
            out_shape=[
                jax.ShapeDtypeStruct((*q.shape[:2], self.heads * HD), BF),
                jax.ShapeDtypeStruct((self.seqs, LEN, 2 * HD), BF),
            ],
            cost_estimate=self._cost(5),
            name="attend_back",
        )(self.place, self.low, self.top, q, o, do, keyval, keyval, self.info, lse_in)


def _hop(v, axis, mask):
    size = lax.axis_size(axis)
    return lax.ppermute(v, axis, [(i, i ^ mask) for i in range(size)])


def _half(rows):
    return rows // 2 // 16 * 16


class Square:
    def __init__(self, blocks):
        self.count = blocks
        me = lax.axis_index("tensor")
        self.place = me ^ jnp.arange(blocks, dtype=jnp.int32)

    def near(self, v):
        return _hop(v, "tensor", 1), _hop(v, "tensor", 2)

    def far(self, v, near):
        h = _half(v.shape[0])
        bx, by = near
        top, bottom = _hop(by[:h], "tensor", 1), _hop(bx[h:], "tensor", 2)
        return jnp.concatenate([v, bx, by, top, bottom], axis=0)

    def gather(self, v):
        return self.far(v, self.near(v))

    def gather_small(self, v):
        blocks = jnp.stack([v] + [_hop(v, "tensor", r) for r in range(1, self.count)])
        return self.ordered(blocks)

    def scatter_small(self, parts):
        parts = self.ordered(parts)
        return parts[0] + sum(_hop(parts[r], "tensor", r) for r in range(1, self.count))

    def begin(self, make):
        corner = make(3).astype(BF)
        h = _half(corner.shape[0])
        return _hop(corner[:h], "tensor", 1), _hop(corner[h:], "tensor", 2)

    def middle(self, begun, make):
        to_y, to_x = begun
        rest = to_x.shape[0]
        h = to_y.shape[0]
        zero = [(0, 0)] * (to_x.ndim - 1)
        py = make(2) + jnp.pad(to_y.astype(F32), [(0, rest)] + zero)
        px = make(1) + jnp.pad(to_x.astype(F32), [(h, 0)] + zero)
        return py.astype(BF), px.astype(BF)

    def finish(self, sums, make):
        py, px = sums
        ry, rx = _hop(py, "tensor", 2), _hop(px, "tensor", 1)
        own = make(0)
        return lambda *others: self._end(own, rx, ry, others)

    def _end(self, own, rx, ry, others):
        if others:
            rx, ry = after((rx, ry), *others)
        return own + rx.astype(F32) + ry.astype(F32)

    def scatter(self, make):
        return self.finish(self.middle(self.begin(make), make), make)()

    def ordered(self, stacked):
        return jnp.take(stacked, self.place, axis=0, mode="clip")


class Plain:
    def __init__(self, blocks):
        self.count = blocks
        self.place = jnp.arange(blocks, dtype=jnp.int32)

    def near(self, v):
        return ()

    def far(self, v, near):
        return lax.all_gather(v, "tensor", axis=0, tiled=True)

    def gather(self, v):
        return self.far(v, ())

    def gather_small(self, v):
        return lax.all_gather(v, "tensor", axis=0)

    def scatter_small(self, parts):
        return lax.psum_scatter(parts, "tensor", scatter_dimension=0)

    def begin(self, make):
        return ()

    def middle(self, begun, make):
        return (jnp.concatenate([make(i).astype(BF) for i in range(self.count)], axis=0),)

    def finish(self, sums, make):
        total = lax.psum_scatter(sums[0], "tensor", scatter_dimension=0, tiled=True).astype(F32)
        return lambda *others: total

    def scatter(self, make):
        return self.finish(self.middle((), make), make)()

    def ordered(self, stacked):
        return stacked


def after(value, *others):
    return lax.optimization_barrier((value, others))[0]


def share_kernel(dp, nt, parts_ref, local_ref, sum_ref, local_sum_ref, got, local_got, sent, came, local_sent, local_came):
    me_dp, me_t = lax.axis_index("dp"), lax.axis_index("tensor")
    count = dp * nt
    barrier = pltpu.get_barrier_semaphore()

    def peer(r):
        return lax.rem(me_dp + r // nt, dp), lax.rem(me_t + lax.rem(r, nt), nt)

    def greet(r, _):
        d, t = peer(r)
        pl.semaphore_signal(barrier, inc=1, device_id=(d, t), device_id_type=pl.DeviceIdType.MESH)
        return 0

    lax.fori_loop(1, count, greet, 0)
    pl.semaphore_wait(barrier, count - 1)

    def part_copy(r):
        d, t = peer(r)
        return pltpu.make_async_remote_copy(
            src_ref=parts_ref.at[d * nt + t],
            dst_ref=got.at[r],
            send_sem=sent.at[r],
            recv_sem=came.at[r],
            device_id=(d, t),
            device_id_type=pl.DeviceIdType.MESH,
        )

    def local_copy(a, slot):
        return pltpu.make_async_remote_copy(
            src_ref=local_ref,
            dst_ref=local_got.at[slot],
            send_sem=local_sent.at[a],
            recv_sem=local_came.at[a],
            device_id=(lax.rem(me_dp + a, dp), me_t),
            device_id_type=pl.DeviceIdType.MESH,
        )

    def send(r, _):
        part_copy(r).start()
        return 0

    def send_local(a, _):
        local_copy(a, me_dp).start()
        return 0

    lax.fori_loop(1, dp, send_local, 0)
    lax.fori_loop(1, count, send, 0)
    local_got[me_dp] = local_ref[...]

    def take(r, total):
        part_copy(r).wait()
        return total + got[r]

    sum_ref[...] = lax.fori_loop(1, count, take, parts_ref[me_dp * nt + me_t])

    def take_local(a, _):
        local_copy(a, lax.rem(me_dp + dp - a, dp)).wait()
        return 0

    lax.fori_loop(1, dp, take_local, 0)
    local_sum_ref[...] = jnp.sum(local_got[...], axis=0)


def share_sums(parts, local):
    dp, nt = lax.axis_size("dp"), lax.axis_size("tensor")
    vmem = pl.BlockSpec(memory_space=pltpu.VMEM)
    return pl.pallas_call(
        functools.partial(share_kernel, dp, nt),
        in_specs=[vmem, vmem],
        out_specs=[vmem, vmem],
        out_shape=[jax.ShapeDtypeStruct(parts.shape[1:], F32), jax.ShapeDtypeStruct(local.shape, F32)],
        scratch_shapes=[
            pltpu.VMEM(parts.shape, F32),
            pltpu.VMEM((dp, *local.shape), F32),
            pltpu.SemaphoreType.DMA((dp * nt,)),
            pltpu.SemaphoreType.DMA((dp * nt,)),
            pltpu.SemaphoreType.DMA((dp,)),
            pltpu.SemaphoreType.DMA((dp,)),
        ],
        compiler_params=pltpu.CompilerParams(collective_id=0, has_side_effects=True),
        name="share_sums",
    )(parts, local)


def norm_parts(v):
    average = jnp.mean(v, axis=-1, keepdims=True)
    centered = v - average
    rate = lax.rsqrt(jnp.mean(centered * centered, axis=-1, keepdims=True) + 1e-05)
    return centered * rate, rate


def norm_back(grad, hat, rate, gain):
    scaled = grad * gain
    return rate * (
        scaled
        - jnp.mean(scaled, axis=-1, keepdims=True)
        - hat * jnp.mean(scaled * hat, axis=-1, keepdims=True)
    )


GELU_A = math.sqrt(2.0 / math.pi)
GELU_B = 0.044715


def gelu_both(a):
    square = a * a
    t = jnp.tanh(GELU_A * (a + GELU_B * square * a))
    half = 0.5 * (1.0 + t)
    slope = half + 0.5 * a * (1.0 - t * t) * (GELU_A * (1.0 + 3.0 * GELU_B * square))
    return a * half, slope


def dot(a, b):
    return jnp.dot(a, b, preferred_element_type=F32)


def dot_t(a, b):
    return lax.dot_general(a, b, (((1,), (1,)), ((), ())), preferred_element_type=F32)


def dot_tokens(a, b):
    return lax.dot_general(a, b, (((0,), (0,)), ((), ())), preferred_element_type=F32)


def per_device(
    tokens,
    segment,
    cotangent,
    ln1_gain,
    ln1_shift,
    w_query,
    b_query,
    w_keyval,
    b_value,
    w_out,
    b_out,
    ln2_gain,
    ln2_shift,
    w_in,
    b_in,
    w_back,
    b_back,
):
    dp, nt = lax.axis_size("dp"), lax.axis_size("tensor")
    rows, width = tokens.shape
    heads = b_query.shape[0] // HD
    wide = heads * HD
    inputs = tokens.astype(F32)
    net = Square(nt) if nt == 4 else Plain(nt)

    hat1, rate1 = norm_parts(inputs)
    normed1 = (hat1 * ln1_gain + ln1_shift).astype(BF)
    n1_near = net.near(normed1)

    keyval_rows = net.gather_small(after(w_keyval.astype(BF), normed1)).reshape(w_query.shape[0], 2 * HD)
    pack = jnp.concatenate([w_query.astype(BF), keyval_rows], axis=1)
    first_full = lax.all_gather(pack, "dp", axis=0, tiled=True)
    output_full = lax.all_gather(w_out.astype(BF), "dp", axis=1, tiled=True)
    inner_full = lax.all_gather(w_in.astype(BF), "dp", axis=0, tiled=True)
    down_full = lax.all_gather(w_back.astype(BF), "dp", axis=1, tiled=True)

    n1 = net.far(normed1, n1_near)
    bias = jnp.concatenate([b_query, jnp.zeros_like(b_value), b_value])
    mixed = (dot(n1, first_full) + bias).astype(BF).reshape(nt, rows, -1)
    seqs = nt * rows // LEN
    keyval = net.ordered(mixed[:, :, wide:]).reshape(seqs, LEN, 2 * HD)
    attention = Attention(segment, net.place, rows, heads)
    cot_near = net.near(after(cotangent, n1))
    mixture, lse = attention.forward(mixed, keyval)
    mixture, cot_near = after((mixture, cot_near))
    attended = net.scatter(lambda i: dot(mixture[i], output_full))
    hidden = inputs + attended + b_out

    def block(whole, i):
        return whole[i * rows : (i + 1) * rows]

    hat2, rate2 = norm_parts(hidden)
    normed2 = (hat2 * ln2_gain + ln2_shift).astype(BF)
    n2 = net.gather(normed2)
    cot = net.far(cotangent, after(cot_near, n2))
    act, slope = gelu_both(dot(n2, inner_full) + b_in)
    act, slope = act.astype(BF), slope.astype(BF)
    down_grad = dot_tokens(act, cot).astype(BF)
    down_total = lax.psum_scatter(down_grad, "dp", scatter_dimension=1, tiled=True).astype(F32)
    pre_grad = (dot_t(after(cot, down_grad), down_full) * slope.astype(F32)).astype(BF)
    second_made = lambda i: dot_t(block(pre_grad, i), inner_full)
    second_sums = net.middle(net.begin(second_made), second_made)
    second_end = net.finish(second_sums, second_made)
    inner_grad = dot_tokens(after(n2, second_sums), pre_grad).astype(BF)
    inner_total = lax.psum_scatter(inner_grad, "dp", scatter_dimension=0, tiled=True).astype(F32)
    inner_bias = jnp.sum(pre_grad, axis=0, dtype=F32)
    feed_all = dot(after(act, inner_grad), down_full).astype(BF)
    second_grad = second_end(feed_all)

    grad_out = cotangent.astype(F32)
    hidden_grad = grad_out + norm_back(second_grad, hat2, rate2, ln2_gain)
    hid = net.gather(hidden_grad.astype(BF))
    mixture_grad = dot_t(hid, output_full).astype(BF).reshape(nt, rows, wide)
    feed_made = lambda i: block(feed_all, i).astype(F32)
    feed_all = after(feed_all, hid)
    feed_begun = net.begin(feed_made)
    mixture_grad, feed_begun = after((mixture_grad, feed_begun), down_total)
    feed_end = net.finish(net.middle(feed_begun, feed_made), feed_made)
    query_low, keyval_part = attention.backward(mixed, mixture, mixture_grad, keyval, lse)
    output_grad = dot_tokens(mixture.reshape(nt * rows, wide), hid).astype(BF)
    output_total = lax.psum_scatter(output_grad, "dp", scatter_dimension=1, tiled=True).astype(F32)
    keyval_part = net.ordered(keyval_part.reshape(nt, rows, 2 * HD))
    mixed_grad = jnp.concatenate([query_low, keyval_part], axis=2)
    feed = feed_end(mixed_grad)
    output = (hidden + feed + b_back).astype(BF)
    mixed_grad = after(mixed_grad, output, inner_total)
    normed_made = lambda i: dot_t(mixed_grad[i], first_full)
    first_grad = dot_tokens(n1, mixed_grad.reshape(nt * rows, -1)).astype(BF)
    first_bias = jnp.sum(mixed_grad, axis=(0, 1), dtype=F32)
    first_total = lax.psum_scatter(first_grad, "dp", scatter_dimension=0, tiled=True)
    query_total = first_total[:, :wide].astype(F32)
    keyval_total = net.scatter_small(first_total[:, wide:].reshape(nt, w_keyval.shape[0], 2 * HD)).astype(F32)
    normed_grad = net.scatter(normed_made)
    tokens_grad = (hidden_grad + norm_back(normed_grad, hat1, rate1, ln1_gain)).astype(BF)

    count = dp * nt
    wide_sums = jnp.stack(
        [
            jnp.sum(normed_grad * hat1, axis=0),
            jnp.sum(normed_grad, axis=0),
            jnp.sum(second_grad * hat2, axis=0),
            jnp.sum(second_grad, axis=0),
            jnp.sum(hidden_grad, axis=0),
            jnp.sum(grad_out, axis=0),
        ]
    )
    kinds, part, value_part = wide_sums.shape[0], width // count, HD // count
    parts = wide_sums.reshape(kinds, count, part).transpose(1, 0, 2).reshape(count, kinds * part)
    parts = jnp.concatenate([parts, first_bias[wide + HD :].reshape(count, value_part)], axis=1)
    lines = pl.cdiv(parts.shape[1], 128)
    parts = jnp.pad(parts, ((0, 0), (0, lines * 128 - parts.shape[1]))).reshape(count, lines, 128)
    local = jnp.concatenate([inner_bias, first_bias[:wide]]).reshape(-1, 128)
    sums, local = share_sums(parts, local)
    sums, local = sums.reshape(-1), local.reshape(-1)
    value_bias = sums[kinds * part : kinds * part + value_part]
    sums = sums[: kinds * part].reshape(kinds, part)
    return (
        output,
        tokens_grad,
        sums[0],
        sums[1],
        query_total,
        local[b_in.shape[0] :],
        keyval_total,
        value_bias,
        output_total,
        sums[4],
        sums[2],
        sums[3],
        inner_total,
        local[: b_in.shape[0]],
        down_total,
        sums[5],
    )


def solution(mesh):
    return jax.shard_map(
        per_device,
        mesh=mesh,
        in_specs=(
            P(("dp", "tensor"), None),
            P("dp"),
            P(("dp", "tensor"), None),
            P(),
            P(),
            P("dp", "tensor"),
            P("tensor"),
            P(("dp", "tensor"), None),
            P(),
            P("tensor", "dp"),
            P(),
            P(),
            P(),
            P("dp", "tensor"),
            P("tensor"),
            P("tensor", "dp"),
            P(),
        ),
        out_specs=(
            P(("dp", "tensor"), None),
            P(("dp", "tensor"), None),
            P(("dp", "tensor")),
            P(("dp", "tensor")),
            P("dp", "tensor"),
            P("tensor"),
            P(("dp", "tensor"), None),
            P(("dp", "tensor")),
            P("tensor", "dp"),
            P(("dp", "tensor")),
            P(("dp", "tensor")),
            P(("dp", "tensor")),
            P("dp", "tensor"),
            P("tensor"),
            P("tensor", "dp"),
            P(("dp", "tensor")),
        ),
        check_vma=False,
    )
```

```python
import functools
import math

import jax
import jax.numpy as jnp
from jax import lax
from jax.experimental import pallas as pl
from jax.experimental.pallas import tpu as pltpu
from jax.sharding import PartitionSpec as P

LEN = 1344
HD = 128
QB = 112
KB = 224
SCALE = 1.0 / math.sqrt(HD)
EXP2 = SCALE * math.log2(math.e)
NEG = -1e30
BF = jnp.bfloat16
F32 = jnp.float32


def _stack(ref, heads):
    return jnp.concatenate([ref[0, :, h * HD : (h + 1) * HD] for h in range(heads)], axis=0)


def _allowed(info_ref, first):
    shape = (KB, info_ref.shape[2])
    place = lax.broadcasted_iota(jnp.int32, shape, 0) + first
    return (place >= info_ref[0, 0:1, :]) & (place <= info_ref[0, 1:2, :])


def _nt(a, b):
    return lax.dot_general(a, b, (((1,), (1,)), ((), ())), preferred_element_type=F32)


def _turn(ref, out):
    for c in range(LEN // KB):
        out[c] = ref[0, c * KB : (c + 1) * KB, :].astype(F32).T.astype(BF)


def attend_kernel(
    heads, per_seq, place_ref, low_ref, top_ref, q_ref, k_ref, v_ref, info_ref, o_ref, lse_ref, s_ref, vt_ref
):
    step = pl.program_id(0)
    low, top = low_ref[step], top_ref[step]

    @pl.when(lax.rem(step, per_seq) == 0)
    def _():
        _turn(v_ref, vt_ref)

    q = _stack(q_ref, heads)
    rows = q.shape[0]

    def score(c, best):
        s = _nt(k_ref[0, pl.ds(pl.multiple_of(c * KB, KB), KB), :], q)
        s = jnp.where(_allowed(info_ref, c * KB), s, NEG)
        s_ref[c] = s
        return jnp.maximum(best, jnp.max(s, axis=0, keepdims=True))

    best = lax.fori_loop(low, top, score, jnp.full((1, rows), NEG, F32))
    shift = best * EXP2

    def mix(c, carry):
        total, acc = carry
        p = jnp.exp2(s_ref[c] * EXP2 - shift)
        total = total + jnp.sum(p, axis=0, keepdims=True)
        acc = acc + jnp.dot(vt_ref[c], p.astype(BF), preferred_element_type=F32)
        return total, acc

    total, acc = lax.fori_loop(
        low, top, mix, (jnp.zeros((1, rows), F32), jnp.zeros((HD, rows), F32))
    )
    out = (acc / total).T.astype(BF)
    for h in range(heads):
        o_ref[0, :, h * HD : (h + 1) * HD] = out[h * QB : (h + 1) * QB]
    lse_ref[0] = jnp.broadcast_to(shift + jnp.log2(total), lse_ref.shape[1:])


def attend_back_kernel(
    heads, per_seq, place_ref, low_ref, top_ref, q_ref, o_ref, do_ref, k_ref, v_ref, info_ref, lse_ref,
    dq_ref, dkv_ref, dk_acc, dv_acc, kt_ref,
):
    step = pl.program_id(0)
    inner = lax.rem(step, per_seq)
    low, top = low_ref[step], top_ref[step]

    @pl.when(inner == 0)
    def _():
        dk_acc[...] = jnp.zeros_like(dk_acc)
        dv_acc[...] = jnp.zeros_like(dv_acc)
        _turn(k_ref, kt_ref)

    q = _stack(q_ref, heads)
    do = _stack(do_ref, heads)
    rows = q.shape[0]
    prod = do.astype(F32) * _stack(o_ref, heads).astype(F32)
    delta = jnp.sum(prod.T, axis=0, keepdims=True)
    lse = lse_ref[0, 0:1, :]

    def body(c, acc):
        window = pl.ds(pl.multiple_of(c * KB, KB), KB)
        s = _nt(k_ref[0, window, :], q)
        s = jnp.where(_allowed(info_ref, c * KB), s * EXP2 - lse, NEG)
        p = jnp.exp2(s)
        dp = _nt(v_ref[0, window, :], do)
        ds = (p * (dp - delta)).astype(BF)
        dv_acc[window, :] += jnp.dot(p.astype(BF), do, preferred_element_type=F32)
        dk_acc[window, :] += jnp.dot(ds, q, preferred_element_type=F32)
        return acc + jnp.dot(kt_ref[c], ds, preferred_element_type=F32)

    acc = lax.fori_loop(low, top, body, jnp.zeros((HD, rows), F32))
    dq = (acc * SCALE).T.astype(BF)
    for h in range(heads):
        dq_ref[0, :, h * HD : (h + 1) * HD] = dq[h * QB : (h + 1) * QB]

    @pl.when(inner == per_seq - 1)
    def _():
        dkv_ref[0, :, :HD] = (dk_acc[...] * SCALE).astype(BF)
        dkv_ref[0, :, HD:] = dv_acc[...].astype(BF)


class Attention:
    def __init__(self, segment, place, rows, heads):
        self.heads, self.rows = heads, rows
        self.seqs = segment.shape[0] // LEN
        self.per_seq = LEN // QB
        self.per_block = rows // QB
        self.steps = self.seqs * self.per_seq
        self.place = place
        seg = segment.reshape(self.seqs, LEN)
        start = jnp.sum((seg[:, None, :] < seg[:, :, None]).astype(jnp.int32), axis=-1)
        pos = jnp.broadcast_to(jnp.arange(LEN, dtype=jnp.int32), seg.shape)
        info = jnp.stack([start, pos], axis=1).reshape(self.seqs, 2, self.per_seq, 1, QB)
        info = jnp.broadcast_to(info, (self.seqs, 2, self.per_seq, heads, QB))
        self.info = info.transpose(0, 2, 1, 3, 4).reshape(self.steps, 2, heads * QB)
        self.low = start.reshape(self.steps, QB)[:, 0] // KB
        last = pos.reshape(self.steps, QB)[:, -1]
        self.top = last // KB + 1

    def _specs(self):
        per_seq, per_block, heads = self.per_seq, self.per_block, self.heads
        wide = heads * HD
        query = pl.BlockSpec((1, QB, wide), lambda i, place, *_: (place[i // per_block], i % per_block, 0))
        key = pl.BlockSpec((1, LEN, HD), lambda i, *_: (i // per_seq, 0, 0))
        value = pl.BlockSpec((1, LEN, HD), lambda i, *_: (i // per_seq, 0, 1))
        info = pl.BlockSpec((1, 2, heads * QB), lambda i, *_: (i, 0, 0))
        lse = pl.BlockSpec((1, 8, heads * QB), lambda i, *_: (i, 0, 0))
        return query, key, value, info, lse

    def _cost(self, products):
        pairs = self.steps * QB * self.heads * LEN // 2
        return pl.CostEstimate(
            flops=2 * pairs * HD * products, transcendentals=pairs, bytes_accessed=8 * self.steps * QB * HD * self.heads
        )

    def forward(self, q, keyval):
        query, key, value, info, lse = self._specs()
        lanes = self.heads * QB
        return pl.pallas_call(
            functools.partial(attend_kernel, self.heads, self.per_seq),
            grid_spec=pltpu.PrefetchScalarGridSpec(
                num_scalar_prefetch=3,
                grid=(self.steps,),
                in_specs=[query, key, value, info],
                out_specs=[query, lse],
                scratch_shapes=[pltpu.VMEM((LEN // KB, KB, lanes), F32), pltpu.VMEM((LEN // KB, HD, KB), BF)],
            ),
            out_shape=[
                jax.ShapeDtypeStruct((*q.shape[:2], self.heads * HD), BF),
                jax.ShapeDtypeStruct((self.steps, 8, lanes), F32),
            ],
            cost_estimate=self._cost(2),
            name="attend",
        )(self.place, self.low, self.top, q, keyval, keyval, self.info)

    def backward(self, q, o, do, keyval, lse_in):
        query, key, value, info, lse = self._specs()
        per_seq = self.per_seq
        return pl.pallas_call(
            functools.partial(attend_back_kernel, self.heads, per_seq),
            grid_spec=pltpu.PrefetchScalarGridSpec(
                num_scalar_prefetch=3,
                grid=(self.steps,),
                in_specs=[query, query, query, key, value, info, lse],
                out_specs=[query, pl.BlockSpec((1, LEN, 2 * HD), lambda i, *_: (i // per_seq, 0, 0))],
                scratch_shapes=[
                    pltpu.VMEM((LEN, HD), F32),
                    pltpu.VMEM((LEN, HD), F32),
                    pltpu.VMEM((LEN // KB, HD, KB), BF),
                ],
            ),
            out_shape=[
                jax.ShapeDtypeStruct((*q.shape[:2], self.heads * HD), BF),
                jax.ShapeDtypeStruct((self.seqs, LEN, 2 * HD), BF),
            ],
            cost_estimate=self._cost(5),
            name="attend_back",
        )(self.place, self.low, self.top, q, o, do, keyval, keyval, self.info, lse_in)


def _hop(v, axis, mask):
    size = lax.axis_size(axis)
    return lax.ppermute(v, axis, [(i, i ^ mask) for i in range(size)])


def _half(rows):
    return rows // 2 // 16 * 16


class Square:
    def __init__(self, blocks):
        self.count = blocks
        me = lax.axis_index("tensor")
        self.place = me ^ jnp.arange(blocks, dtype=jnp.int32)

    def near(self, v):
        return _hop(v, "tensor", 1), _hop(v, "tensor", 2)

    def far(self, v, near, *others):
        h = _half(v.shape[0])
        bx, by = near
        pieces = _hop(by[:h], "tensor", 1), _hop(bx[h:], "tensor", 2)
        top, bottom = after(pieces, *others) if others else pieces
        return jnp.concatenate([v, bx, by, top, bottom], axis=0)

    def gather(self, v):
        return self.far(v, self.near(v))

    def gather_small(self, v):
        blocks = jnp.stack([v] + [_hop(v, "tensor", r) for r in range(1, self.count)])
        return self.ordered(blocks)

    def corner(self, make):
        return make(3, 1).astype(BF)

    def begin(self, corner):
        h = _half(corner.shape[0])
        return _hop(corner[:h], "tensor", 1), _hop(corner[h:], "tensor", 2)

    def middle(self, begun, make):
        to_y, to_x = begun
        h, rest = to_y.shape[0], to_x.shape[0]
        edge = jnp.concatenate([to_x, to_y], axis=0).astype(F32)
        pair = (make(1, 2) + jnp.pad(edge, [(h, rest)] + [(0, 0)] * (edge.ndim - 1))).astype(BF)
        return pair[: h + rest], pair[h + rest :]

    def tails(self, sums):
        px, py = sums
        return _hop(px, "tensor", 1), _hop(py, "tensor", 2)

    def end(self, own, tails):
        return own + tails[0].astype(F32) + tails[1].astype(F32)

    def own(self, make):
        return make(0, 1)

    def scatter(self, make):
        begun = self.begin(self.corner(make))
        own = self.own(make)
        return self.end(own, self.tails(self.middle(after(begun, own), make)))

    def ordered(self, stacked):
        return jnp.take(stacked, self.place, axis=0, mode="clip")


class Plain:
    def __init__(self, blocks):
        self.count = blocks
        self.place = jnp.arange(blocks, dtype=jnp.int32)

    def near(self, v):
        return ()

    def far(self, v, near, *others):
        return lax.all_gather(v, "tensor", axis=0, tiled=True)

    def gather(self, v):
        return self.far(v, ())

    def gather_small(self, v):
        return lax.all_gather(v, "tensor", axis=0)

    def corner(self, make):
        return ()

    def begin(self, corner):
        return ()

    def middle(self, begun, make):
        return (make(0, self.count).astype(BF),)

    def tails(self, sums):
        return lax.psum_scatter(sums[0], "tensor", scatter_dimension=0, tiled=True)

    def end(self, own, tails):
        return tails.astype(F32)

    def own(self, make):
        return ()

    def scatter(self, make):
        return self.end((), self.tails(self.middle((), make)))

    def ordered(self, stacked):
        return stacked


def after(value, *others):
    return lax.optimization_barrier((value, others))[0]


def share_kernel(
    dp, nt, parts_ref, local_ref, group_ref, sum_ref, local_sum_ref, group_sum_ref,
    got, local_got, group_got, sent, came, local_sent, local_came, group_sent, group_came,
):
    me_dp, me_t = lax.axis_index("dp"), lax.axis_index("tensor")
    count = dp * nt
    barrier = pltpu.get_barrier_semaphore()

    def peer(r):
        return lax.rem(me_dp + r // nt, dp), lax.rem(me_t + lax.rem(r, nt), nt)

    def greet(r, _):
        d, t = peer(r)
        pl.semaphore_signal(barrier, inc=1, device_id=(d, t), device_id_type=pl.DeviceIdType.MESH)
        return 0

    lax.fori_loop(1, count, greet, 0)
    pl.semaphore_wait(barrier, count - 1)

    def part_copy(r):
        d, t = peer(r)
        return pltpu.make_async_remote_copy(
            src_ref=parts_ref.at[d * nt + t],
            dst_ref=got.at[r],
            send_sem=sent.at[r],
            recv_sem=came.at[r],
            device_id=(d, t),
            device_id_type=pl.DeviceIdType.MESH,
        )

    def local_copy(a, slot):
        return pltpu.make_async_remote_copy(
            src_ref=local_ref,
            dst_ref=local_got.at[slot],
            send_sem=local_sent.at[a],
            recv_sem=local_came.at[a],
            device_id=(lax.rem(me_dp + a, dp), me_t),
            device_id_type=pl.DeviceIdType.MESH,
        )

    def group_copy(b):
        t = lax.rem(me_t + b, nt)
        return pltpu.make_async_remote_copy(
            src_ref=group_ref.at[t],
            dst_ref=group_got.at[b],
            send_sem=group_sent.at[b],
            recv_sem=group_came.at[b],
            device_id=(me_dp, t),
            device_id_type=pl.DeviceIdType.MESH,
        )

    def send(r, _):
        part_copy(r).start()
        return 0

    def send_local(a, _):
        local_copy(a, me_dp).start()
        return 0

    def send_group(b, _):
        group_copy(b).start()
        return 0

    lax.fori_loop(1, nt, send_group, 0)
    lax.fori_loop(1, dp, send_local, 0)
    lax.fori_loop(1, count, send, 0)
    local_got[me_dp] = local_ref[...]

    def take(r, total):
        part_copy(r).wait()
        return total + got[r]

    sum_ref[...] = lax.fori_loop(1, count, take, parts_ref[me_dp * nt + me_t])

    def take_local(a, _):
        local_copy(a, lax.rem(me_dp + dp - a, dp)).wait()
        return 0

    lax.fori_loop(1, dp, take_local, 0)
    local_sum_ref[...] = jnp.sum(local_got[...], axis=0)

    def take_group(b, total):
        group_copy(b).wait()
        return total + group_got[b]

    group_sum_ref[...] = lax.fori_loop(1, nt, take_group, group_ref[me_t])


def share_sums(parts, local, group):
    dp, nt = lax.axis_size("dp"), lax.axis_size("tensor")
    vmem = pl.BlockSpec(memory_space=pltpu.VMEM)
    return pl.pallas_call(
        functools.partial(share_kernel, dp, nt),
        in_specs=[vmem, vmem, vmem],
        out_specs=[vmem, vmem, vmem],
        out_shape=[jax.ShapeDtypeStruct(v, F32) for v in (parts.shape[1:], local.shape, group.shape[1:])],
        scratch_shapes=[
            pltpu.VMEM(parts.shape, F32),
            pltpu.VMEM((dp, *local.shape), F32),
            pltpu.VMEM(group.shape, F32),
            pltpu.SemaphoreType.DMA((dp * nt,)),
            pltpu.SemaphoreType.DMA((dp * nt,)),
            pltpu.SemaphoreType.DMA((dp,)),
            pltpu.SemaphoreType.DMA((dp,)),
            pltpu.SemaphoreType.DMA((nt,)),
            pltpu.SemaphoreType.DMA((nt,)),
        ],
        compiler_params=pltpu.CompilerParams(collective_id=0, has_side_effects=True),
        name="share_sums",
    )(parts, local, group)


def norm_parts(v):
    average = jnp.mean(v, axis=-1, keepdims=True)
    centered = v - average
    rate = lax.rsqrt(jnp.mean(centered * centered, axis=-1, keepdims=True) + 1e-05)
    return centered * rate, rate


def norm_back(grad, hat, rate, gain):
    scaled = grad * gain
    return rate * (
        scaled
        - jnp.mean(scaled, axis=-1, keepdims=True)
        - hat * jnp.mean(scaled * hat, axis=-1, keepdims=True)
    )


GELU_A = math.sqrt(2.0 / math.pi)
GELU_B = 0.044715


def gelu_both(a):
    square = a * a
    t = jnp.tanh(GELU_A * (a + GELU_B * square * a))
    half = 0.5 * (1.0 + t)
    slope = half + 0.5 * a * (1.0 - t * t) * (GELU_A * (1.0 + 3.0 * GELU_B * square))
    return a * half, slope


def dot(a, b):
    return jnp.dot(a, b, preferred_element_type=F32)


def dot_t(a, b):
    return lax.dot_general(a, b, (((1,), (1,)), ((), ())), preferred_element_type=F32)


def dot_tokens(a, b):
    return lax.dot_general(a, b, (((0,), (0,)), ((), ())), preferred_element_type=F32)


def per_device(
    tokens,
    segment,
    cotangent,
    ln1_gain,
    ln1_shift,
    w_query,
    b_query,
    w_keyval,
    b_value,
    w_out,
    b_out,
    ln2_gain,
    ln2_shift,
    w_in,
    b_in,
    w_back,
    b_back,
):
    dp, nt = lax.axis_size("dp"), lax.axis_size("tensor")
    rows, width = tokens.shape
    heads = b_query.shape[0] // HD
    wide = heads * HD
    inputs = tokens.astype(F32)
    net = Square(nt) if nt == 4 else Plain(nt)

    hat1, rate1 = norm_parts(inputs)
    normed1 = (hat1 * ln1_gain + ln1_shift).astype(BF)
    n1_near = net.near(normed1)

    keyval_rows = net.gather_small(after(w_keyval.astype(BF), normed1)).reshape(w_query.shape[0], 2 * HD)
    n1_near = after(n1_near, keyval_rows)
    pack = jnp.concatenate([w_query.astype(BF), keyval_rows], axis=1)
    first_full = lax.all_gather(pack, "dp", axis=0, tiled=True)
    output_full = lax.all_gather(w_out.astype(BF), "dp", axis=1, tiled=True)
    inner_full = lax.all_gather(w_in.astype(BF), "dp", axis=0, tiled=True)
    down_full = lax.all_gather(w_back.astype(BF), "dp", axis=1, tiled=True)

    n1 = net.far(normed1, n1_near)
    bias = jnp.concatenate([b_query, jnp.zeros_like(b_value), b_value])
    queries = (dot(n1, first_full) + bias).astype(BF).reshape(nt, rows, -1)
    keyval = net.ordered(queries[:, :, wide:]).reshape(nt * rows // LEN, LEN, 2 * HD)
    attention = Attention(segment, net.place, rows, heads)
    cot_near = net.near(after(cotangent, n1))
    mixture, lse = attention.forward(queries, keyval)
    mixture, cot_near = after((mixture, cot_near))

    def block(whole, i, n):
        return whole[i * rows : (i + n) * rows]

    mixture = mixture.reshape(nt * rows, wide)
    attended = net.scatter(lambda i, n: dot(block(mixture, i, n), output_full))
    hidden = inputs + attended + b_out

    hat2, rate2 = norm_parts(hidden)
    normed2 = (hat2 * ln2_gain + ln2_shift).astype(BF)
    n2 = net.gather(normed2)
    act, slope = gelu_both(dot(n2, inner_full) + b_in)
    act, slope = act.astype(BF), slope.astype(BF)
    cot = net.far(cotangent, after(cot_near, n2), act)
    down_grad = dot_tokens(act, cot).astype(BF)
    down_low = lax.psum_scatter(down_grad, "dp", scatter_dimension=1, tiled=True)
    pre_grad = (dot_t(after(cot, down_grad), down_full) * slope.astype(F32)).astype(BF)
    second_made = lambda i, n: dot_t(block(pre_grad, i, n), inner_full)
    second_begun = net.begin(net.corner(second_made))
    second_own = net.own(second_made)
    second_sums = net.middle(after(second_begun, second_own), second_made)
    second_tails = net.tails(second_sums)
    inner_grad = dot_tokens(after(n2, second_sums), pre_grad).astype(BF)
    second_grad = net.end(second_own, after(second_tails, inner_grad))

    grad_out = cotangent.astype(F32)
    hidden_grad = grad_out + norm_back(second_grad, hat2, rate2, ln2_gain)
    hidden_low = hidden_grad.astype(BF)
    hidden_near = net.near(hidden_low)
    inner_low = lax.psum_scatter(after(inner_grad, hidden_low), "dp", scatter_dimension=0, tiled=True)
    feed_all = dot(after(act, hidden_low), down_full).astype(BF)
    inner_bias = jnp.sum(after(pre_grad, hidden_low), axis=0, dtype=F32)
    hid = net.far(hidden_low, after(hidden_near, feed_all))
    mixture_grad = dot_t(hid, output_full).astype(BF).reshape(nt, rows, wide)
    feed_made = lambda i, n: block(feed_all, i, n).astype(F32)
    feed_all = after(feed_all, hid)
    feed_begun = net.begin(net.corner(feed_made))
    mixture_grad, feed_begun, down_low = after((mixture_grad, feed_begun, down_low))
    feed_tails = net.tails(net.middle(feed_begun, feed_made))
    query_low, keyval_part = attention.backward(queries, mixture.reshape(nt, rows, wide), mixture_grad, keyval, lse)
    output_grad = dot_tokens(mixture, hid).astype(BF)
    output_low = lax.psum_scatter(output_grad, "dp", scatter_dimension=1, tiled=True)
    keyval_part = net.ordered(keyval_part.reshape(nt, rows, 2 * HD))
    mixed_grad = jnp.concatenate([query_low, keyval_part], axis=2).reshape(nt * rows, wide + 2 * HD)
    mixed_grad, feed_tails, inner_low = after((mixed_grad, feed_tails, inner_low))
    output = (hidden + net.end(net.own(feed_made), feed_tails) + b_back).astype(BF)
    normed_made = lambda i, n: dot_t(block(mixed_grad, i, n), first_full)
    normed_corner = net.corner(normed_made)
    first_grad = dot_tokens(after(n1, normed_corner), mixed_grad).astype(BF)
    normed_own = net.own(normed_made)
    normed_sums = net.middle(after(net.begin(normed_corner), first_grad, normed_own), normed_made)
    first_bias = jnp.sum(after(mixed_grad, normed_sums), axis=0, dtype=F32)
    first_total = lax.psum_scatter(after(first_grad, normed_sums), "dp", scatter_dimension=0, tiled=True)
    query_total = first_total[:, :wide].astype(F32)
    keyval_total = first_total[:, wide:].astype(F32).reshape(nt, w_keyval.shape[0], 2 * HD)
    normed_grad = net.end(normed_own, net.tails(normed_sums))
    tokens_grad = (hidden_grad + norm_back(normed_grad, hat1, rate1, ln1_gain)).astype(BF)
    down_total, inner_total, output_total = (v.astype(F32) for v in (down_low, inner_low, output_low))

    count = dp * nt
    wide_sums = jnp.stack(
        [
            jnp.sum(normed_grad * hat1, axis=0),
            jnp.sum(normed_grad, axis=0),
            jnp.sum(second_grad * hat2, axis=0),
            jnp.sum(second_grad, axis=0),
            jnp.sum(hidden_grad, axis=0),
            jnp.sum(grad_out, axis=0),
        ]
    )
    kinds, part, value_part = wide_sums.shape[0], width // count, HD // count
    parts = wide_sums.reshape(kinds, count, part).transpose(1, 0, 2).reshape(count, kinds * part)
    parts = jnp.concatenate([parts, first_bias[wide + HD :].reshape(count, value_part)], axis=1)
    lines = pl.cdiv(parts.shape[1], 128)
    parts = jnp.pad(parts, ((0, 0), (0, lines * 128 - parts.shape[1]))).reshape(count, lines, 128)
    local = jnp.concatenate([inner_bias, first_bias[:wide]]).reshape(-1, 128)
    sums, local, keyval_total = share_sums(parts, local, keyval_total)
    sums, local = sums.reshape(-1), local.reshape(-1)
    value_bias = sums[kinds * part : kinds * part + value_part]
    sums = sums[: kinds * part].reshape(kinds, part)
    return (
        output,
        tokens_grad,
        sums[0],
        sums[1],
        query_total,
        local[b_in.shape[0] :],
        keyval_total,
        value_bias,
        output_total,
        sums[4],
        sums[2],
        sums[3],
        inner_total,
        local[: b_in.shape[0]],
        down_total,
        sums[5],
    )


def solution(mesh):
    return jax.shard_map(
        per_device,
        mesh=mesh,
        in_specs=(
            P(("dp", "tensor"), None),
            P("dp"),
            P(("dp", "tensor"), None),
            P(),
            P(),
            P("dp", "tensor"),
            P("tensor"),
            P(("dp", "tensor"), None),
            P(),
            P("tensor", "dp"),
            P(),
            P(),
            P(),
            P("dp", "tensor"),
            P("tensor"),
            P("tensor", "dp"),
            P(),
        ),
        out_specs=(
            P(("dp", "tensor"), None),
            P(("dp", "tensor"), None),
            P(("dp", "tensor")),
            P(("dp", "tensor")),
            P("dp", "tensor"),
            P("tensor"),
            P(("dp", "tensor"), None),
            P(("dp", "tensor")),
            P("tensor", "dp"),
            P(("dp", "tensor")),
            P(("dp", "tensor")),
            P(("dp", "tensor")),
            P("dp", "tensor"),
            P("tensor"),
            P("tensor", "dp"),
            P(("dp", "tensor")),
        ),
        check_vma=False,
    )
```

```python
import functools
import math

import jax
import jax.numpy as jnp
from jax import lax
from jax.experimental import pallas as pl
from jax.experimental.pallas import tpu as pltpu
from jax.sharding import PartitionSpec as P

LEN = 1344
HD = 128
QB = 112
KB = 224
SCALE = 1.0 / math.sqrt(HD)
EXP2 = SCALE * math.log2(math.e)
NEG = -1e30
BF = jnp.bfloat16
F32 = jnp.float32


def _stack(ref, heads):
    return jnp.concatenate([ref[0, :, h * HD : (h + 1) * HD] for h in range(heads)], axis=0)


def _allowed(info_ref, first):
    shape = (KB, info_ref.shape[2])
    place = lax.broadcasted_iota(jnp.int32, shape, 0) + first
    return (place >= info_ref[0, 0:1, :]) & (place <= info_ref[0, 1:2, :])


def _nt(a, b):
    return lax.dot_general(a, b, (((1,), (1,)), ((), ())), preferred_element_type=F32)


def _turn(ref, out):
    for c in range(LEN // KB):
        out[c] = ref[0, c * KB : (c + 1) * KB, :].astype(F32).T.astype(BF)


def attend_kernel(
    heads, per_seq, place_ref, low_ref, top_ref, q_ref, k_ref, v_ref, info_ref, o_ref, lse_ref, s_ref, vt_ref
):
    step = pl.program_id(0)
    low, top = low_ref[step], top_ref[step]

    @pl.when(lax.rem(step, per_seq) == 0)
    def _():
        _turn(v_ref, vt_ref)

    q = _stack(q_ref, heads)
    rows = q.shape[0]

    def score(c, best):
        s = _nt(k_ref[0, pl.ds(pl.multiple_of(c * KB, KB), KB), :], q)
        s = jnp.where(_allowed(info_ref, c * KB), s, NEG)
        s_ref[c] = s
        return jnp.maximum(best, jnp.max(s, axis=0, keepdims=True))

    best = lax.fori_loop(low, top, score, jnp.full((1, rows), NEG, F32))
    shift = best * EXP2

    def mix(c, carry):
        total, acc = carry
        p = jnp.exp2(s_ref[c] * EXP2 - shift)
        total = total + jnp.sum(p, axis=0, keepdims=True)
        acc = acc + jnp.dot(vt_ref[c], p.astype(BF), preferred_element_type=F32)
        return total, acc

    total, acc = lax.fori_loop(
        low, top, mix, (jnp.zeros((1, rows), F32), jnp.zeros((HD, rows), F32))
    )
    out = (acc / total).T.astype(BF)
    for h in range(heads):
        o_ref[0, :, h * HD : (h + 1) * HD] = out[h * QB : (h + 1) * QB]
    lse_ref[0] = jnp.broadcast_to(shift + jnp.log2(total), lse_ref.shape[1:])


def attend_back_kernel(
    heads, per_seq, place_ref, low_ref, top_ref, q_ref, o_ref, do_ref, k_ref, v_ref, info_ref, lse_ref,
    dq_ref, dkv_ref, dk_acc, dv_acc, kt_ref,
):
    step = pl.program_id(0)
    inner = lax.rem(step, per_seq)
    low, top = low_ref[step], top_ref[step]

    @pl.when(inner == 0)
    def _():
        dk_acc[...] = jnp.zeros_like(dk_acc)
        dv_acc[...] = jnp.zeros_like(dv_acc)
        _turn(k_ref, kt_ref)

    q = _stack(q_ref, heads)
    do = _stack(do_ref, heads)
    rows = q.shape[0]
    prod = do.astype(F32) * _stack(o_ref, heads).astype(F32)
    delta = jnp.sum(prod.T, axis=0, keepdims=True)
    lse = lse_ref[0, 0:1, :]

    def body(c, acc):
        window = pl.ds(pl.multiple_of(c * KB, KB), KB)
        s = _nt(k_ref[0, window, :], q)
        s = jnp.where(_allowed(info_ref, c * KB), s * EXP2 - lse, NEG)
        p = jnp.exp2(s)
        dp = _nt(v_ref[0, window, :], do)
        ds = (p * (dp - delta)).astype(BF)
        dv_acc[window, :] += jnp.dot(p.astype(BF), do, preferred_element_type=F32)
        dk_acc[window, :] += jnp.dot(ds, q, preferred_element_type=F32)
        return acc + jnp.dot(kt_ref[c], ds, preferred_element_type=F32)

    acc = lax.fori_loop(low, top, body, jnp.zeros((HD, rows), F32))
    dq = (acc * SCALE).T.astype(BF)
    for h in range(heads):
        dq_ref[0, :, h * HD : (h + 1) * HD] = dq[h * QB : (h + 1) * QB]

    @pl.when(inner == per_seq - 1)
    def _():
        dkv_ref[0, :, :HD] = (dk_acc[...] * SCALE).astype(BF)
        dkv_ref[0, :, HD:] = dv_acc[...].astype(BF)


class Attention:
    def __init__(self, segment, place, rows, heads):
        self.heads, self.rows = heads, rows
        self.seqs = segment.shape[0] // LEN
        self.per_seq = LEN // QB
        self.per_block = rows // QB
        self.steps = self.seqs * self.per_seq
        self.place = place
        seg = segment.reshape(self.seqs, LEN)
        start = jnp.sum((seg[:, None, :] < seg[:, :, None]).astype(jnp.int32), axis=-1)
        pos = jnp.broadcast_to(jnp.arange(LEN, dtype=jnp.int32), seg.shape)
        info = jnp.stack([start, pos], axis=1).reshape(self.seqs, 2, self.per_seq, 1, QB)
        info = jnp.broadcast_to(info, (self.seqs, 2, self.per_seq, heads, QB))
        self.info = info.transpose(0, 2, 1, 3, 4).reshape(self.steps, 2, heads * QB)
        self.low = start.reshape(self.steps, QB)[:, 0] // KB
        last = pos.reshape(self.steps, QB)[:, -1]
        self.top = last // KB + 1

    def _specs(self):
        per_seq, per_block, heads = self.per_seq, self.per_block, self.heads
        wide = heads * HD
        query = pl.BlockSpec((1, QB, wide), lambda i, place, *_: (place[i // per_block], i % per_block, 0))
        key = pl.BlockSpec((1, LEN, HD), lambda i, *_: (i // per_seq, 0, 0))
        value = pl.BlockSpec((1, LEN, HD), lambda i, *_: (i // per_seq, 0, 1))
        info = pl.BlockSpec((1, 2, heads * QB), lambda i, *_: (i, 0, 0))
        lse = pl.BlockSpec((1, 8, heads * QB), lambda i, *_: (i, 0, 0))
        return query, key, value, info, lse

    def _cost(self, products):
        pairs = self.steps * QB * self.heads * LEN // 2
        return pl.CostEstimate(
            flops=2 * pairs * HD * products, transcendentals=pairs, bytes_accessed=8 * self.steps * QB * HD * self.heads
        )

    def forward(self, q, keyval):
        query, key, value, info, lse = self._specs()
        lanes = self.heads * QB
        return pl.pallas_call(
            functools.partial(attend_kernel, self.heads, self.per_seq),
            grid_spec=pltpu.PrefetchScalarGridSpec(
                num_scalar_prefetch=3,
                grid=(self.steps,),
                in_specs=[query, key, value, info],
                out_specs=[query, lse],
                scratch_shapes=[pltpu.VMEM((LEN // KB, KB, lanes), F32), pltpu.VMEM((LEN // KB, HD, KB), BF)],
            ),
            out_shape=[
                jax.ShapeDtypeStruct((*q.shape[:2], self.heads * HD), BF),
                jax.ShapeDtypeStruct((self.steps, 8, lanes), F32),
            ],
            cost_estimate=self._cost(2),
            name="attend",
        )(self.place, self.low, self.top, q, keyval, keyval, self.info)

    def backward(self, q, o, do, keyval, lse_in):
        query, key, value, info, lse = self._specs()
        per_seq = self.per_seq
        return pl.pallas_call(
            functools.partial(attend_back_kernel, self.heads, per_seq),
            grid_spec=pltpu.PrefetchScalarGridSpec(
                num_scalar_prefetch=3,
                grid=(self.steps,),
                in_specs=[query, query, query, key, value, info, lse],
                out_specs=[query, pl.BlockSpec((1, LEN, 2 * HD), lambda i, *_: (i // per_seq, 0, 0))],
                scratch_shapes=[
                    pltpu.VMEM((LEN, HD), F32),
                    pltpu.VMEM((LEN, HD), F32),
                    pltpu.VMEM((LEN // KB, HD, KB), BF),
                ],
            ),
            out_shape=[
                jax.ShapeDtypeStruct((*q.shape[:2], self.heads * HD), BF),
                jax.ShapeDtypeStruct((self.seqs, LEN, 2 * HD), BF),
            ],
            cost_estimate=self._cost(5),
            name="attend_back",
        )(self.place, self.low, self.top, q, o, do, keyval, keyval, self.info, lse_in)


def _hop(v, axis, mask):
    size = lax.axis_size(axis)
    return lax.ppermute(v, axis, [(i, i ^ mask) for i in range(size)])


def _half(rows):
    return rows // 2 // 16 * 16


def square_kernel(v_ref, out_ref, local, sent, came):
    me_dp, me_t = lax.axis_index("dp"), lax.axis_index("tensor")
    rows = v_ref.shape[0]
    h = _half(rows)
    column = lax.rem(me_t, 2)
    beside = me_t + 1 - 2 * column
    across = lax.rem(me_t + 2, 4)
    top, bottom = pl.ds(0, h), pl.ds(h, rows - h)
    barrier = pltpu.get_barrier_semaphore()
    for t in (beside, across):
        pl.semaphore_signal(barrier, inc=1, device_id=(me_dp, t), device_id_type=pl.DeviceIdType.MESH)
    pl.semaphore_wait(barrier, 2)

    def copy(slot, src, block, part, t):
        return pltpu.make_async_remote_copy(
            src_ref=src,
            dst_ref=out_ref.at[block, part],
            send_sem=sent.at[slot],
            recv_sem=came.at[slot],
            device_id=(me_dp, t),
            device_id_type=pl.DeviceIdType.MESH,
        )

    first_x = copy(0, v_ref.at[bottom], 1, bottom, beside)
    first_y = copy(1, v_ref.at[top], 2, top, across)
    second_x = copy(2, v_ref.at[top], 1, top, beside)
    second_y = copy(3, v_ref.at[bottom], 2, bottom, across)
    own = pltpu.make_async_copy(v_ref, out_ref.at[0], local)
    for c in (first_x, first_y, second_x, second_y, own):
        c.start()
    on_x = copy(4, out_ref.at[2, top], 3, top, beside)
    on_y = copy(5, out_ref.at[1, bottom], 3, bottom, across)
    first_y.wait_recv()
    on_x.start()
    first_x.wait_recv()
    on_y.start()
    first_x.wait_send()
    first_y.wait_send()
    for c in (second_x, second_y, on_x, on_y, own):
        c.wait()


def square_gather(v):
    rows, width = v.shape
    whole = pl.pallas_call(
        square_kernel,
        in_specs=[pl.BlockSpec(memory_space=pltpu.VMEM)],
        out_specs=pl.BlockSpec(memory_space=pl.ANY),
        out_shape=jax.ShapeDtypeStruct((4, rows, width), v.dtype),
        scratch_shapes=[
            pltpu.SemaphoreType.DMA(()),
            pltpu.SemaphoreType.DMA((6,)),
            pltpu.SemaphoreType.DMA((6,)),
        ],
        compiler_params=pltpu.CompilerParams(collective_id=1, has_side_effects=True),
        cost_estimate=pl.CostEstimate(flops=0, bytes_accessed=100 * v.size, transcendentals=0),
        name="square_gather",
    )(v)
    return whole.reshape(4 * rows, width)


class Square:
    def __init__(self, blocks):
        self.count = blocks
        me = lax.axis_index("tensor")
        self.place = me ^ jnp.arange(blocks, dtype=jnp.int32)

    def near(self, v):
        return _hop(v, "tensor", 1), _hop(v, "tensor", 2)

    def halves(self, near):
        h = _half(near[0].shape[0])
        return near[1][:h], near[0][h:]

    def far(self, v, near, halves=None, *others):
        bx, by = near
        to_y, to_x = self.halves(near) if halves is None else halves
        pieces = _hop(to_y, "tensor", 1), _hop(to_x, "tensor", 2)
        top, bottom = after(pieces, *others) if others else pieces
        return jnp.concatenate([v, bx, by, top, bottom], axis=0)

    def gather(self, v):
        return self.far(v, self.near(v))

    def gather_now(self, v):
        return square_gather(v)

    def gather_small(self, v):
        blocks = jnp.stack([v] + [_hop(v, "tensor", r) for r in range(1, self.count)])
        return self.ordered(blocks)

    def corner(self, make):
        return make(3, 1).astype(BF)

    def begin(self, corner):
        h = _half(corner.shape[0])
        return _hop(corner[:h], "tensor", 1), _hop(corner[h:], "tensor", 2)

    def middle(self, begun, make):
        to_y, to_x = begun
        h, rest = to_y.shape[0], to_x.shape[0]
        edge = jnp.concatenate([to_x, to_y], axis=0).astype(F32)
        pair = (make(1, 2) + jnp.pad(edge, [(h, rest)] + [(0, 0)] * (edge.ndim - 1))).astype(BF)
        return pair[: h + rest], pair[h + rest :]

    def tails(self, sums):
        px, py = sums
        return _hop(px, "tensor", 1), _hop(py, "tensor", 2)

    def end(self, own, tails):
        return own + tails[0].astype(F32) + tails[1].astype(F32)

    def own(self, make):
        return make(0, 1)

    def scatter(self, make):
        begun = self.begin(self.corner(make))
        own = self.own(make)
        return self.end(own, self.tails(self.middle(after(begun, own), make)))

    def ordered(self, stacked):
        return jnp.take(stacked, self.place, axis=0, mode="clip")


class Plain:
    def __init__(self, blocks):
        self.count = blocks
        self.place = jnp.arange(blocks, dtype=jnp.int32)

    def near(self, v):
        return ()

    def halves(self, near):
        return ()

    def far(self, v, near, halves=None, *others):
        return lax.all_gather(v, "tensor", axis=0, tiled=True)

    def gather(self, v):
        return self.far(v, ())

    def gather_now(self, v):
        return self.far(v, ())

    def gather_small(self, v):
        return lax.all_gather(v, "tensor", axis=0)

    def corner(self, make):
        return ()

    def begin(self, corner):
        return ()

    def middle(self, begun, make):
        return (make(0, self.count).astype(BF),)

    def tails(self, sums):
        return lax.psum_scatter(sums[0], "tensor", scatter_dimension=0, tiled=True)

    def end(self, own, tails):
        return tails.astype(F32)

    def own(self, make):
        return ()

    def scatter(self, make):
        return self.end((), self.tails(self.middle((), make)))

    def ordered(self, stacked):
        return stacked


def after(value, *others):
    return lax.optimization_barrier((value, others))[0]


def share_kernel(
    dp, nt, parts_ref, local_ref, group_ref, sum_ref, local_sum_ref, group_sum_ref,
    got, local_got, group_got, sent, came, local_sent, local_came, group_sent, group_came,
):
    me_dp, me_t = lax.axis_index("dp"), lax.axis_index("tensor")
    count = dp * nt
    barrier = pltpu.get_barrier_semaphore()

    def peer(r):
        return lax.rem(me_dp + r // nt, dp), lax.rem(me_t + lax.rem(r, nt), nt)

    def greet(r, _):
        d, t = peer(r)
        pl.semaphore_signal(barrier, inc=1, device_id=(d, t), device_id_type=pl.DeviceIdType.MESH)
        return 0

    lax.fori_loop(1, count, greet, 0)
    pl.semaphore_wait(barrier, count - 1)

    def part_copy(r):
        d, t = peer(r)
        return pltpu.make_async_remote_copy(
            src_ref=parts_ref.at[d * nt + t],
            dst_ref=got.at[r],
            send_sem=sent.at[r],
            recv_sem=came.at[r],
            device_id=(d, t),
            device_id_type=pl.DeviceIdType.MESH,
        )

    def local_copy(a, slot):
        return pltpu.make_async_remote_copy(
            src_ref=local_ref,
            dst_ref=local_got.at[slot],
            send_sem=local_sent.at[a],
            recv_sem=local_came.at[a],
            device_id=(lax.rem(me_dp + a, dp), me_t),
            device_id_type=pl.DeviceIdType.MESH,
        )

    def group_copy(b):
        t = lax.rem(me_t + b, nt)
        return pltpu.make_async_remote_copy(
            src_ref=group_ref.at[t],
            dst_ref=group_got.at[b],
            send_sem=group_sent.at[b],
            recv_sem=group_came.at[b],
            device_id=(me_dp, t),
            device_id_type=pl.DeviceIdType.MESH,
        )

    def send(r, _):
        part_copy(r).start()
        return 0

    def send_local(a, _):
        local_copy(a, me_dp).start()
        return 0

    def send_group(b, _):
        group_copy(b).start()
        return 0

    lax.fori_loop(1, nt, send_group, 0)
    lax.fori_loop(1, dp, send_local, 0)
    lax.fori_loop(1, count, send, 0)
    local_got[me_dp] = local_ref[...]

    def take(r, total):
        part_copy(r).wait()
        return total + got[r]

    sum_ref[...] = lax.fori_loop(1, count, take, parts_ref[me_dp * nt + me_t])

    def take_local(a, _):
        local_copy(a, lax.rem(me_dp + dp - a, dp)).wait()
        return 0

    lax.fori_loop(1, dp, take_local, 0)
    local_sum_ref[...] = jnp.sum(local_got[...], axis=0)

    def take_group(b, total):
        group_copy(b).wait()
        return total + group_got[b]

    group_sum_ref[...] = lax.fori_loop(1, nt, take_group, group_ref[me_t])


def share_sums(parts, local, group):
    dp, nt = lax.axis_size("dp"), lax.axis_size("tensor")
    vmem = pl.BlockSpec(memory_space=pltpu.VMEM)
    return pl.pallas_call(
        functools.partial(share_kernel, dp, nt),
        in_specs=[vmem, vmem, vmem],
        out_specs=[vmem, vmem, vmem],
        out_shape=[jax.ShapeDtypeStruct(v, F32) for v in (parts.shape[1:], local.shape, group.shape[1:])],
        scratch_shapes=[
            pltpu.VMEM(parts.shape, F32),
            pltpu.VMEM((dp, *local.shape), F32),
            pltpu.VMEM(group.shape, F32),
            pltpu.SemaphoreType.DMA((dp * nt,)),
            pltpu.SemaphoreType.DMA((dp * nt,)),
            pltpu.SemaphoreType.DMA((dp,)),
            pltpu.SemaphoreType.DMA((dp,)),
            pltpu.SemaphoreType.DMA((nt,)),
            pltpu.SemaphoreType.DMA((nt,)),
        ],
        compiler_params=pltpu.CompilerParams(collective_id=0, has_side_effects=True),
        name="share_sums",
    )(parts, local, group)


def norm_parts(v):
    average = jnp.mean(v, axis=-1, keepdims=True)
    centered = v - average
    rate = lax.rsqrt(jnp.mean(centered * centered, axis=-1, keepdims=True) + 1e-05)
    return centered * rate, rate


def norm_back(grad, hat, rate, gain):
    scaled = grad * gain
    return rate * (
        scaled
        - jnp.mean(scaled, axis=-1, keepdims=True)
        - hat * jnp.mean(scaled * hat, axis=-1, keepdims=True)
    )


GELU_A = math.sqrt(2.0 / math.pi)
GELU_B = 0.044715


def gelu_both(a):
    square = a * a
    t = jnp.tanh(GELU_A * (a + GELU_B * square * a))
    half = 0.5 * (1.0 + t)
    slope = half + 0.5 * a * (1.0 - t * t) * (GELU_A * (1.0 + 3.0 * GELU_B * square))
    return a * half, slope


def dot(a, b):
    return jnp.dot(a, b, preferred_element_type=F32)


def dot_t(a, b):
    return lax.dot_general(a, b, (((1,), (1,)), ((), ())), preferred_element_type=F32)


def dot_tokens(a, b):
    return lax.dot_general(a, b, (((0,), (0,)), ((), ())), preferred_element_type=F32)


def per_device(
    tokens,
    segment,
    cotangent,
    ln1_gain,
    ln1_shift,
    w_query,
    b_query,
    w_keyval,
    b_value,
    w_out,
    b_out,
    ln2_gain,
    ln2_shift,
    w_in,
    b_in,
    w_back,
    b_back,
):
    dp, nt = lax.axis_size("dp"), lax.axis_size("tensor")
    rows, width = tokens.shape
    heads = b_query.shape[0] // HD
    wide = heads * HD
    inputs = tokens.astype(F32)
    net = Square(nt) if nt == 4 else Plain(nt)

    hat1, rate1 = norm_parts(inputs)
    normed1 = (hat1 * ln1_gain + ln1_shift).astype(BF)

    keyval_rows = net.gather_small(w_keyval.astype(BF)).reshape(w_query.shape[0], 2 * HD)
    pack = jnp.concatenate([w_query.astype(BF), keyval_rows], axis=1)
    first_full = lax.all_gather(pack, "dp", axis=0, tiled=True)
    n1_near = net.near(normed1)
    output_full = lax.all_gather(w_out.astype(BF), "dp", axis=1, tiled=True)
    inner_full = lax.all_gather(w_in.astype(BF), "dp", axis=0, tiled=True)
    down_full = lax.all_gather(w_back.astype(BF), "dp", axis=1, tiled=True)

    n1 = net.far(normed1, n1_near)
    bias = jnp.concatenate([b_query, jnp.zeros_like(b_value), b_value])
    queries = (dot(n1, first_full) + bias).astype(BF).reshape(nt, rows, -1)
    keyval = net.ordered(queries[:, :, wide:]).reshape(nt * rows // LEN, LEN, 2 * HD)
    attention = Attention(segment, net.place, rows, heads)
    cot_near = net.near(after(cotangent, n1))
    mixture, lse = attention.forward(queries, keyval)
    mixture, cot_near = after((mixture, cot_near))
    cot_halves = net.halves(cot_near)

    def block(whole, i, n):
        return whole[i * rows : (i + n) * rows]

    mixture = mixture.reshape(nt * rows, wide)
    attended = net.scatter(lambda i, n: dot(block(mixture, i, n), output_full))
    hidden = inputs + attended + b_out

    hat2, rate2 = norm_parts(hidden)
    normed2 = (hat2 * ln2_gain + ln2_shift).astype(BF)
    n2 = net.gather_now(normed2)
    cot_halves = after(cot_halves, n2)
    act, slope = gelu_both(dot(n2, inner_full) + b_in)
    act, slope = act.astype(BF), slope.astype(BF)
    cot = net.far(cotangent, cot_near, cot_halves, act)
    down_grad = dot_tokens(act, cot).astype(BF)
    down_low = lax.psum_scatter(down_grad, "dp", scatter_dimension=1, tiled=True)
    pre_grad = (dot_t(after(cot, down_grad), down_full) * slope.astype(F32)).astype(BF)
    second_made = lambda i, n: dot_t(block(pre_grad, i, n), inner_full)
    second_begun = net.begin(net.corner(second_made))
    second_own = net.own(second_made)
    second_sums = net.middle(after(second_begun, second_own), second_made)
    second_tails = net.tails(second_sums)
    inner_grad = dot_tokens(after(n2, second_sums), pre_grad).astype(BF)
    second_grad = net.end(second_own, after(second_tails, inner_grad))

    grad_out = cotangent.astype(F32)
    hidden_grad = grad_out + norm_back(second_grad, hat2, rate2, ln2_gain)
    hidden_low = hidden_grad.astype(BF)
    hidden_near = net.near(hidden_low)
    inner_low = lax.psum_scatter(after(inner_grad, hidden_low), "dp", scatter_dimension=0, tiled=True)
    feed_all = dot(after(act, hidden_low), down_full).astype(BF)
    inner_bias = jnp.sum(after(pre_grad, hidden_low), axis=0, dtype=F32)
    hid = net.far(hidden_low, after(hidden_near, feed_all))
    mixture_grad = dot_t(hid, output_full).astype(BF).reshape(nt, rows, wide)
    feed_made = lambda i, n: block(feed_all, i, n).astype(F32)
    feed_all = after(feed_all, hid)
    feed_begun = net.begin(net.corner(feed_made))
    mixture_grad, feed_begun, down_low = after((mixture_grad, feed_begun, down_low))
    feed_tails = net.tails(net.middle(feed_begun, feed_made))
    query_low, keyval_part = attention.backward(queries, mixture.reshape(nt, rows, wide), mixture_grad, keyval, lse)
    output_grad = dot_tokens(mixture, hid).astype(BF)
    output_low = lax.psum_scatter(output_grad, "dp", scatter_dimension=1, tiled=True)
    keyval_part = net.ordered(keyval_part.reshape(nt, rows, 2 * HD))
    mixed_grad = jnp.concatenate([query_low, keyval_part], axis=2).reshape(nt * rows, wide + 2 * HD)
    mixed_grad, feed_tails, inner_low = after((mixed_grad, feed_tails, inner_low))
    output = (hidden + net.end(net.own(feed_made), feed_tails) + b_back).astype(BF)
    normed_made = lambda i, n: dot_t(block(mixed_grad, i, n), first_full)
    normed_corner = net.corner(normed_made)
    first_grad = dot_tokens(after(n1, normed_corner), mixed_grad).astype(BF)
    normed_own = net.own(normed_made)
    normed_sums = net.middle(after(net.begin(normed_corner), first_grad, normed_own), normed_made)
    first_bias = jnp.sum(after(mixed_grad, normed_sums), axis=0, dtype=F32)
    first_total = lax.psum_scatter(after(first_grad, normed_sums), "dp", scatter_dimension=0, tiled=True)
    query_total = first_total[:, :wide].astype(F32)
    keyval_total = first_total[:, wide:].astype(F32).reshape(nt, w_keyval.shape[0], 2 * HD)
    normed_grad = net.end(normed_own, net.tails(normed_sums))
    tokens_grad = (hidden_grad + norm_back(normed_grad, hat1, rate1, ln1_gain)).astype(BF)
    down_total, inner_total, output_total = (v.astype(F32) for v in (down_low, inner_low, output_low))

    count = dp * nt
    wide_sums = jnp.stack(
        [
            jnp.sum(normed_grad * hat1, axis=0),
            jnp.sum(normed_grad, axis=0),
            jnp.sum(second_grad * hat2, axis=0),
            jnp.sum(second_grad, axis=0),
            jnp.sum(hidden_grad, axis=0),
            jnp.sum(grad_out, axis=0),
        ]
    )
    kinds, part, value_part = wide_sums.shape[0], width // count, HD // count
    parts = wide_sums.reshape(kinds, count, part).transpose(1, 0, 2).reshape(count, kinds * part)
    parts = jnp.concatenate([parts, first_bias[wide + HD :].reshape(count, value_part)], axis=1)
    lines = pl.cdiv(parts.shape[1], 128)
    parts = jnp.pad(parts, ((0, 0), (0, lines * 128 - parts.shape[1]))).reshape(count, lines, 128)
    local = jnp.concatenate([inner_bias, first_bias[:wide]]).reshape(-1, 128)
    sums, local, keyval_total = share_sums(parts, local, keyval_total)
    sums, local = sums.reshape(-1), local.reshape(-1)
    value_bias = sums[kinds * part : kinds * part + value_part]
    sums = sums[: kinds * part].reshape(kinds, part)
    return (
        output,
        tokens_grad,
        sums[0],
        sums[1],
        query_total,
        local[b_in.shape[0] :],
        keyval_total,
        value_bias,
        output_total,
        sums[4],
        sums[2],
        sums[3],
        inner_total,
        local[: b_in.shape[0]],
        down_total,
        sums[5],
    )


def solution(mesh):
    return jax.shard_map(
        per_device,
        mesh=mesh,
        in_specs=(
            P(("dp", "tensor"), None),
            P("dp"),
            P(("dp", "tensor"), None),
            P(),
            P(),
            P("dp", "tensor"),
            P("tensor"),
            P(("dp", "tensor"), None),
            P(),
            P("tensor", "dp"),
            P(),
            P(),
            P(),
            P("dp", "tensor"),
            P("tensor"),
            P("tensor", "dp"),
            P(),
        ),
        out_specs=(
            P(("dp", "tensor"), None),
            P(("dp", "tensor"), None),
            P(("dp", "tensor")),
            P(("dp", "tensor")),
            P("dp", "tensor"),
            P("tensor"),
            P(("dp", "tensor"), None),
            P(("dp", "tensor")),
            P("tensor", "dp"),
            P(("dp", "tensor")),
            P(("dp", "tensor")),
            P(("dp", "tensor")),
            P("dp", "tensor"),
            P("tensor"),
            P("tensor", "dp"),
            P(("dp", "tensor")),
        ),
        check_vma=False,
    )
```
